256 devices in a mesh: sec: 2 (over core), row: 4 (over x), col: 32 (over z, y).
Axes of the slice: x: 4, y: 4, z: 8, core: 2. Of those that a mesh axis runs over, the one named last changes fastest.
Arguments:
- leaf_rhs: bfloat16 [2, 4, 1, 32, 128, 256], P('sec', 'row', None, 'col'), may hold values from -6 to 6
- sep_rhs: bfloat16 [2, 4, 32, 128, 256], P('sec', 'row', 'col'), may hold values from -6 to 6
- top_rhs: bfloat16 [4, 32, 128, 256], P('row', 'col'), may hold values from -6 to 6
- leaf_inv: float32 [2, 4, 1, 32, 128, 128], P('sec', 'row', None, 'col'), may hold values from -1 to 3, as said below
- sep_inv: float32 [2, 4, 32, 128, 128], P('sec', 'row', 'col'), may hold values from -1 to 3, as said below
- top_inv: float32 [4, 32, 128, 128], P('row', 'col'), may hold values from -1 to 3, as said below
- sep_leaf: bfloat16 [2, 4, 32, 128, 4, 1, 32, 128], P('sec', 'row', None, None, None, None, 'col'), may hold values from -0.0625 to 0.0625
- top_leaf: bfloat16 [2, 4, 32, 128, 4, 1, 32, 128], P('sec', 'row', None, None, None, None, 'col'), may hold values from -0.046875 to 0.046875
- top_sep: bfloat16 [2, 4, 32, 128, 4, 32, 128], P('sec', 'row', None, None, None, 'col'), may hold values from -0.046875 to 0.046875
- sep_leaf_mask: int32 [2, 4, 32, 4, 1, 32], P('sec', 'row', None, None, None, 'col'), may hold values 0 or 1
- top_leaf_mask: int32 [2, 4, 32, 4, 1, 32], P('sec', 'row', None, None, None, 'col'), may hold values 0 or 1
- top_sep_mask: int32 [2, 4, 32, 4, 32], P('sec', 'row', None, None, 'col'), may hold values 0 or 1
Outputs:
- leaf_x: float32 [2, 4, 1, 32, 128, 256], P('sec', 'row', None, 'col')
- sep_x: float32 [2, 4, 32, 128, 256], P('sec', 'row', 'col')
- top_x: float32 [4, 32, 128, 256], P('row', 'col')
The draws below stay inside these ranges and needn't reach their ends.
Inputs may be any that keep to these rules, and one draw needn't show every extreme that they name: `leaf_inv`: every 128 x 128 block is lower triangular with positive diagonal. `sep_inv`: every 128 x 128 block is lower triangular with positive diagonal. `top_inv`: every 128 x 128 block is lower triangular with positive diagonal.
All inputs are finite; a program needn't handle non-finite values. No bound on the sum of `sep_leaf_mask` or of `top_leaf_mask` or of `top_sep_mask` on one device may be relied on, other than what follows from the above.
Results may differ from the reference program's by a relative error of at most 0.0036.
Values may be sent and summed in bfloat16 or wider, within the bound.
A program may use at most 128 MiB of HBM per device.

```python
import math
import jax
import jax.numpy as jnp
from jax import lax

W = 128
NRHS = 256
LEAF_DEV = 1
NLEAF = 128
NSEP = 128
N_SEC = 2
N_ROW = 4
N_COL = 32


def triangle_blocks(key, leading):
    key_diag, key_below = jax.random.split(key)
    full_shape = leading + (W, W)
    lower_part = (lax.broadcasted_iota(jnp.int32, (W, W), 0) > lax.broadcasted_iota(jnp.int32, (W, W), 1)).astype(jnp.float32)
    on_diag = (lax.broadcasted_iota(jnp.int32, (W, W), 0) == lax.broadcasted_iota(jnp.int32, (W, W), 1)).astype(jnp.float32)
    diagonal = jax.random.uniform(key_diag, leading + (W, 1), jnp.float32, 0.6, 1.5)
    spread = jnp.clip(jax.random.normal(key_below, full_shape, jnp.float32), -4.0, 4.0) * (0.6 / math.sqrt(W))
    return spread * lower_part + diagonal * on_diag


def draw_leaf_inv(key, part):
    return triangle_blocks(key, (N_SEC, N_ROW, LEAF_DEV, N_COL))


def draw_sep_inv(key, part):
    return triangle_blocks(key, (N_SEC, N_ROW, N_COL))


def draw_top_inv(key, part):
    return triangle_blocks(key, (N_ROW, N_COL))


def place_ends(drawn, stream_key, smallest, high):
    spot = [jax.random.randint(jax.random.fold_in(stream_key, axis), (), 0, length) for axis, length in enumerate(drawn.shape)]
    main_axis = drawn.shape.index(max(drawn.shape))
    beside = spot[:main_axis] + [(spot[main_axis] + 1) % drawn.shape[main_axis]] + spot[main_axis + 1:]
    return drawn.at[tuple(spot)].set(smallest).at[tuple(beside)].set(high)


def block_scale(rng, extent, cuts, least, top_value):
    factor_of = 1.0
    for position, parts in cuts:
        draws = jax.random.uniform(jax.random.fold_in(jax.random.fold_in(rng, 6), position), (parts,), jnp.float32, least / len(cuts), top_value / len(cuts))
        factor_of = factor_of * jnp.repeat(jnp.exp(draws), extent[position] // parts).reshape((-1,) + (1,) * (len(extent) - 1 - position))
    return factor_of


def scatter_about(rng, shape, width, limit, cuts=(), dtype=jnp.bfloat16):
    result = jax.random.normal(rng, shape, jnp.float32) * width
    if len(cuts) > 0:
        result = block_scale(rng, shape, cuts, -0.22, 0.18) * result
    return jnp.clip(result, min=-limit, max=limit).astype(dtype)


def setup_inputs(seed: int = 0) -> dict:
    streams_of = jax.random.split(jax.random.key(seed), 13)
    leaf_rhs = scatter_about(streams_of[0], (N_SEC, N_ROW, LEAF_DEV, N_COL, W, NRHS), 1.0, 6.0, ((0, 2), (1, 4), (3, 32)))
    sep_rhs = scatter_about(streams_of[1], (N_SEC, N_ROW, N_COL, W, NRHS), 1.0, 6.0, ((0, 2), (1, 4), (2, 32)))
    top_rhs = scatter_about(streams_of[2], (N_ROW, N_COL, W, NRHS), 1.0, 6.0, ((0, 4), (1, 32)))
    leaf_inv = draw_leaf_inv(jax.random.fold_in(streams_of[12], 71), 0)
    sep_inv = draw_sep_inv(jax.random.fold_in(streams_of[12], 71), 0)
    top_inv = draw_top_inv(jax.random.fold_in(streams_of[12], 71), 0)
    sep_leaf = scatter_about(streams_of[6], (N_SEC, N_ROW, N_COL, W, N_ROW, LEAF_DEV, N_COL, W), (W * NLEAF // 2) ** -0.5, 0.0625, ((0, 2), (1, 4), (6, 32)))
    top_leaf = scatter_about(streams_of[7], (N_SEC, N_ROW, N_COL, W, N_ROW, LEAF_DEV, N_COL, W), (W * NLEAF) ** -0.5, 0.046875, ((0, 2), (1, 4), (6, 32)))
    top_sep = scatter_about(streams_of[8], (N_SEC, N_ROW, N_COL, W, N_ROW, N_COL, W), (W * NSEP) ** -0.5, 0.046875, ((0, 2), (1, 4), (5, 32)))
    sep_leaf_mask = place_ends((jax.random.randint(streams_of[9], (N_SEC, N_ROW, N_COL, N_ROW, LEAF_DEV, N_COL), 0, 2) < 1).astype(jnp.int32), jax.random.fold_in(streams_of[9], 1), 0, 1)
    top_leaf_mask = place_ends((jax.random.randint(streams_of[10], (N_SEC, N_ROW, N_COL, N_ROW, LEAF_DEV, N_COL), 0, 2) < 1).astype(jnp.int32), jax.random.fold_in(streams_of[10], 1), 0, 1)
    top_sep_mask = place_ends((jax.random.randint(streams_of[11], (N_SEC, N_ROW, N_COL, N_ROW, N_COL), 0, 2) < 1).astype(jnp.int32), jax.random.fold_in(streams_of[11], 1), 0, 1)
    return {"leaf_rhs": leaf_rhs, "sep_rhs": sep_rhs, "top_rhs": top_rhs, "leaf_inv": leaf_inv, "sep_inv": sep_inv, "top_inv": top_inv, "sep_leaf": sep_leaf, "top_leaf": top_leaf, "top_sep": top_sep, "sep_leaf_mask": sep_leaf_mask, "top_leaf_mask": top_leaf_mask, "top_sep_mask": top_sep_mask}


def lower_apply(inverse, right_side):
    return jnp.einsum("...ab,...bn->...an", inverse, right_side, precision=lax.Precision.HIGHEST)


def upper_apply(inverse, right_side):
    return jnp.einsum("...ba,...bn->...an", inverse, right_side, precision=lax.Precision.HIGHEST)


def reference(leaf_rhs, sep_rhs, top_rhs, leaf_inv, sep_inv, top_inv, sep_leaf, top_leaf, top_sep, sep_leaf_mask, top_leaf_mask, top_sep_mask):
    node_rows = N_ROW * N_COL * W
    leaf_rows = N_ROW * LEAF_DEV * N_COL * W
    contract = (((0,), (0,)), ((), ()))

    def masked_leaf(tile_set, pattern):
        weights = pattern.astype(jnp.bfloat16)[:, :, None, :, :, :, None]
        return (tile_set * weights).reshape(node_rows, leaf_rows)

    def masked_cross(tile_set, pattern):
        weights = pattern.astype(jnp.bfloat16)[:, :, None, :, :, None]
        return (tile_set * weights).reshape(node_rows, node_rows)

    def forward(section):
        rhs_leaf, inv_leaf, rhs_sep, inv_sep, tiles_sl, tiles_tl, tiles_ts, mask_sl, mask_tl, mask_ts = section
        leaf_y = lower_apply(inv_leaf, rhs_leaf.astype(jnp.float32))
        leaf_flat = leaf_y.astype(jnp.bfloat16).reshape(leaf_rows, NRHS)
        sep_sum = jnp.dot(masked_leaf(tiles_sl, mask_sl), leaf_flat, preferred_element_type=jnp.float32)
        sep_y = lower_apply(inv_sep, rhs_sep.astype(jnp.float32) - sep_sum.reshape(N_ROW, N_COL, W, NRHS))
        sep_flat = sep_y.astype(jnp.bfloat16).reshape(node_rows, NRHS)
        top_part = jnp.dot(masked_leaf(tiles_tl, mask_tl), leaf_flat, preferred_element_type=jnp.float32)
        top_part = top_part + jnp.dot(masked_cross(tiles_ts, mask_ts), sep_flat, preferred_element_type=jnp.float32)
        return leaf_y, sep_y, top_part

    leaf_y, sep_y, top_parts = lax.map(forward, (leaf_rhs, leaf_inv, sep_rhs, sep_inv, sep_leaf, top_leaf, top_sep, sep_leaf_mask, top_leaf_mask, top_sep_mask))
    top_sum = jnp.sum(top_parts, axis=0).reshape(N_ROW, N_COL, W, NRHS)
    top_y = lower_apply(top_inv, top_rhs.astype(jnp.float32) - top_sum)
    top_x = upper_apply(top_inv, top_y)
    top_flat = top_x.astype(jnp.bfloat16).reshape(node_rows, NRHS)

    def backward(section):
        sep_y_s, leaf_y_s, inv_sep, inv_leaf, tiles_sl, tiles_tl, tiles_ts, mask_sl, mask_tl, mask_ts = section
        sep_t = lax.dot_general(masked_cross(tiles_ts, mask_ts), top_flat, contract, preferred_element_type=jnp.float32)
        sep_x = upper_apply(inv_sep, sep_y_s - sep_t.reshape(N_ROW, N_COL, W, NRHS))
        sep_flat = sep_x.astype(jnp.bfloat16).reshape(node_rows, NRHS)
        leaf_t = lax.dot_general(masked_leaf(tiles_sl, mask_sl), sep_flat, contract, preferred_element_type=jnp.float32)
        leaf_t = leaf_t + lax.dot_general(masked_leaf(tiles_tl, mask_tl), top_flat, contract, preferred_element_type=jnp.float32)
        leaf_x = upper_apply(inv_leaf, leaf_y_s - leaf_t.reshape(N_ROW, LEAF_DEV, N_COL, W, NRHS))
        return leaf_x, sep_x

    leaf_x, sep_x = lax.map(backward, (sep_y, leaf_y, sep_inv, leaf_inv, sep_leaf, top_leaf, top_sep, sep_leaf_mask, top_leaf_mask, top_sep_mask))
    return leaf_x, sep_x, top_x
```

```python
import functools

import jax
import jax.numpy as jnp
from jax import lax
from jax.experimental import pallas as pl
from jax.experimental.pallas import tpu as pltpu
from jax.sharding import PartitionSpec as P

MESH = pl.DeviceIdType.MESH
NY = 4
BF = jnp.bfloat16
F32 = jnp.float32
HI = lax.Precision.HIGHEST


def kernel(
    NX,
    NZ,
    leaf_rhs,
    sep_rhs,
    top_rhs,
    leaf_inv,
    sep_inv,
    top_inv,
    sl_hbm,
    tl_hbm,
    ts_hbm,
    sl_mask,
    tl_mask,
    ts_mask,
    leaf_out,
    sep_out,
    top_out,
    raw,
    tiles,
    select,
    leaf_y,
    sep_y,
    leaf_all,
    sep_all,
    part,
    top_part,
    swap_out,
    swap_in,
    fa_send,
    fa_recv,
    fb_send,
    fb_recv,
    fz_send,
    fz_recv,
    ta_send,
    ta_recv,
    tb_send,
    tb_recv,
    tz_send,
    tz_recv,
    top_full,
    top_all,
    sepx_all,
    acc_sep,
    acc_leaf,
    xr_send,
    xr_recv,
    load_sem,
    xg_ss,
    xg_rs,
    xr_ss,
    xr_rs,
    a_ss,
    a_rs,
    b_ss,
    b_rs,
    z_ss,
    z_rs,
    swap_ss,
    swap_rs,
    ga_ss,
    ga_rs,
    gb_ss,
    gb_rs,
    gz_ss,
    gz_rs,
    pair_ss,
    pair_rs,
    full_ss,
    full_rs,
):
    W = 128
    NC = NY * NZ
    s = lax.axis_index("sec")
    x = lax.axis_index("row")
    c = lax.axis_index("col")
    z = c // NY
    y = c % NY

    def col_of(yy, zz):
        return zz * NY + yy

    y_up = lax.rem(y + 1, NY)
    y_far = lax.rem(y + 2, NY)
    y_dn = lax.rem(y + 3, NY)
    to_up = (s, x, col_of(y_up, z))
    to_dn = (s, x, col_of(y_dn, z))
    to_pair = (1 - s, x, c)

    def to_x(o):
        return (s, lax.rem(x + o, NX), c)

    def to_z(zz):
        return (s, x, col_of(y, zz))

    def order(k):
        half = (k + 1) // 2
        return NZ // 2 + half * (1 - 2 * lax.rem(k, 2))

    def remote(src, dst, ss, rs, dev):
        return pltpu.make_async_remote_copy(
            src_ref=src,
            dst_ref=dst,
            send_sem=ss,
            recv_sem=rs,
            device_id=dev,
            device_id_type=MESH,
        )

    loads = [
        pltpu.make_async_copy(ref, raw.at[t], load_sem.at[t])
        for t, ref in enumerate((sl_hbm, tl_hbm, ts_hbm))
    ]
    for load in loads:
        load.start()

    barrier = pltpu.get_barrier_semaphore()

    def greet(dev):
        pl.semaphore_signal(barrier, inc=1, device_id=dev, device_id_type=MESH)

    greet(to_pair)
    for o in range(1, NX):
        greet(to_x(o))
    greet(to_up)
    greet(to_dn)
    for o in range(1, NZ):
        greet(to_z(lax.rem(z + o, NZ)))

    ly = jnp.dot(leaf_inv[...], leaf_rhs[...].astype(F32), precision=HI, preferred_element_type=F32)
    leaf_y[...] = ly
    leaf_all[x] = ly.astype(BF)

    pl.semaphore_wait(barrier, NX + NZ + 1)

    def x_gather(p, buf):
        return [
            remote(buf.at[x], buf.at[x], xg_ss.at[p, o], xg_rs.at[p, o], to_x(o))
            for o in range(1, NX)
        ]

    leaf_sends = x_gather(0, leaf_all)
    for copy in leaf_sends:
        copy.start()

    SB = 64
    rows_i = lax.broadcasted_iota(jnp.int32, (SB * NX, SB * NX), 0)
    cols_i = lax.broadcasted_iota(jnp.int32, (SB * NX, SB * NX), 1)
    wanted = lax.rem(rows_i, SB) * NX + rows_i // SB
    select[...] = jnp.where(cols_i == wanted, 1.0, 0.0).astype(BF)

    def prep(t, mask, lo, n):
        def unit(i, carry):
            cc = lo + i
            yy = lax.rem(cc, NY)
            zz = cc // NY
            for sub in range(W // SB):
                start = pl.multiple_of(cc * (W * NX) + sub * (SB * NX), SB * NX)
                block = raw[t, pl.ds(start, SB * NX), :]
                moved = jnp.dot(select[...], block, preferred_element_type=F32)
                row = pl.multiple_of(zz * W + sub * SB, SB)
                for r in range(NX):
                    keep = mask[r, 0, cc].astype(F32)
                    tiles[t, yy, pl.ds(row, SB), r * W : (r + 1) * W] = (
                        moved[r * SB : (r + 1) * SB] * keep
                    ).astype(BF)
            return carry

        lax.fori_loop(0, n, unit, 0)

    loads[0].wait()
    prep(0, sl_mask, 0, NC)

    for copy in leaf_sends:
        copy.wait()

    MB = min(512, NZ * W)

    def forward(t, values, yy, write):
        def block(i, carry):
            row = pl.multiple_of(i * MB, MB)
            out = jnp.dot(
                tiles[t, yy, pl.ds(row, MB), :],
                values[...].reshape(NX * W, 2 * W),
                preferred_element_type=F32,
            )
            write(row, out)
            return carry

        lax.fori_loop(0, NZ * W // MB, block, 0)

    def sep_dot(yy):
        def write(row, out):
            part[yy, pl.ds(row, MB), :] = out

        forward(0, leaf_all, yy, write)

    H = W // 2

    def reduce_col(p, chunk, start_more, work, a_s, a_r, b_s, b_r, z_s, z_r):
        def zp_of(k):
            return lax.rem(z + order(k), NZ)

        def a_copies(k):
            return (
                remote(a_s.at[k, 0:H], a_r.at[0, k], a_ss.at[p, 0, k], a_rs.at[p, 0, k], to_up),
                remote(a_s.at[k, H:W], a_r.at[1, k], a_ss.at[p, 1, k], a_rs.at[p, 1, k], to_dn),
            )

        def b_copies(k):
            return (
                remote(b_s.at[0, k], b_r.at[0, k], b_ss.at[p, 0, k], b_rs.at[p, 0, k], to_up),
                remote(b_s.at[1, k], b_r.at[1, k], b_ss.at[p, 1, k], b_rs.at[p, 1, k], to_dn),
            )

        def z_copy(k):
            return remote(z_s.at[k], z_r.at[k], z_ss.at[p, k], z_rs.at[p, k], to_z(zp_of(k)))

        def send_a(k):
            a_s[k] = chunk(y_far, zp_of(k), 0, W).astype(BF)
            for copy in a_copies(k):
                copy.start()

        def send_b(k):
            zp = zp_of(k)
            up, dn = a_copies(k)
            cup, cdn = b_copies(k)
            b_s[0, k, H:W] = chunk(y_up, zp, H, H).astype(BF)
            b_s[1, k, 0:H] = chunk(y_dn, zp, 0, H).astype(BF)
            up.wait_recv()
            b_s[0, k, 0:H] = (chunk(y_up, zp, 0, H) + a_r[0, k].astype(F32)).astype(BF)
            cup.start()
            dn.wait_recv()
            b_s[1, k, H:W] = (chunk(y_dn, zp, H, H) + a_r[1, k].astype(F32)).astype(BF)
            cdn.start()

        def total(k):
            for copy in b_copies(k):
                copy.wait_recv()
            return chunk(y, zp_of(k), 0, W) + b_r[0, k].astype(F32) + b_r[1, k].astype(F32)

        def send_z(k):
            z_s[k] = total(k).astype(BF)
            z_copy(k).start()

        send_a(0)
        send_a(1)
        start_more()

        def step(k, carry):
            @pl.when(k < NZ - 2)
            def _():
                send_a(k + 2)

            send_b(k)
            work(k)

            @pl.when(k >= 2)
            def _():
                send_z(k - 2)

            return carry

        lax.fori_loop(0, NZ, step, 0)
        send_z(NZ - 2)
        out = total(NZ - 1)
        for k in range(NZ - 1):
            z_copy(k).wait_recv()
            out = out + z_r[k].astype(F32)

        def drain():
            def one(k, carry):
                for copy in a_copies(k) + b_copies(k):
                    copy.wait_send()

                @pl.when(k < NZ - 1)
                def _():
                    z_copy(k).wait_send()

                return carry

            lax.fori_loop(0, NZ, one, 0)

        return out, drain

    sep_dot(y_far)

    def sep_more():
        sep_dot(y_up)
        sep_dot(y_dn)
        sep_dot(y)

    def sep_chunk(yy, zp, lo, n):
        return part[yy, pl.ds(pl.multiple_of(zp * W + lo, n), n), :]

    per = max(1, 2 * NC // NZ)
    split = NZ // 2

    def top_leaf_dot(yy):
        def write(row, out):
            top_part[0, yy, pl.ds(row, MB), :] = out[:, 0:W]
            top_part[1, yy, pl.ds(row, MB), :] = out[:, W : 2 * W]

        forward(1, leaf_all, yy, write)

    def sep_work(k):
        @pl.when(k == 0)
        def _():
            loads[1].wait()
            loads[2].wait()

        @pl.when(k < split)
        def _():
            prep(1, tl_mask, k * per, per)

        @pl.when(k >= split)
        def _():
            prep(2, ts_mask, (k - split) * per, per)

        @pl.when(k == split)
        def _():
            top_leaf_dot(y)
            top_leaf_dot(y_up)

        @pl.when(k == NZ - 1)
        def _():
            top_leaf_dot(y_dn)
            top_leaf_dot(y_far)

    sep_sum, drain_sep = reduce_col(
        0, sep_chunk, sep_more, sep_work, fa_send, fa_recv, fb_send, fb_recv, fz_send, fz_recv
    )
    sy = jnp.dot(
        sep_inv[...],
        sep_rhs[...].astype(F32) - sep_sum,
        precision=HI,
        preferred_element_type=F32,
    )
    sep_y[...] = sy
    sep_all[x] = sy.astype(BF)
    sep_sends = x_gather(1, sep_all)
    for copy in sep_sends:
        copy.start()
    drain_sep()
    for copy in sep_sends:
        copy.wait()

    order_y = (y_far, y_up, y_dn, y)

    def swap_copy(i):
        return remote(
            swap_out.at[i], swap_in.at[i], swap_ss.at[i], swap_rs.at[i], to_pair
        )

    for i, yy in enumerate(order_y):

        def write(row, out, i=i, yy=yy):
            top_part[0, yy, pl.ds(row, MB), :] += out[:, 0:W]
            top_part[1, yy, pl.ds(row, MB), :] += out[:, W : 2 * W]
            swap_out[i, pl.ds(row, MB), :] = top_part[1 - s, yy, pl.ds(row, MB), :].astype(BF)

        forward(2, sep_all, yy, write)
        swap_copy(i).start()

    def join(i, yy):
        swap_copy(i).wait()

        def block(j, carry):
            row = pl.multiple_of(j * W, W)
            top_part[s, yy, pl.ds(row, W), :] += swap_in[i, pl.ds(row, W), :].astype(F32)
            return carry

        lax.fori_loop(0, NZ, block, 0)

    join(0, y_far)

    def top_more():
        join(1, y_up)
        join(2, y_dn)
        join(3, y)

    def top_chunk(yy, zp, lo, n):
        return top_part[s, yy, pl.ds(pl.multiple_of(zp * W + lo, n), n), :]

    top_sum, drain_top = reduce_col(
        1, top_chunk, top_more, lambda k: None, ta_send, ta_recv, tb_send, tb_recv, tz_send, tz_recv
    )
    mine = pl.ds(pl.multiple_of(s * W, W), W)
    ty = jnp.dot(
        top_inv[...],
        top_rhs[:, mine].astype(F32) - top_sum,
        precision=HI,
        preferred_element_type=F32,
    )
    tx = jnp.dot(ty.T, top_inv[...], precision=HI, preferred_element_type=F32)
    top_full[mine, :] = tx
    top_all[y, z, mine, :] = tx.astype(BF)

    def gather_col(p, buf, lo, rows, start_more, arrived, use):
        def zp_of(k):
            return lax.rem(z + NZ - order(NZ - 1 - k), NZ)

        def at(yy, zz, first, n):
            return buf.at[yy, zz, pl.ds(pl.multiple_of(lo + first, n), n)]

        half = rows // 2

        def z_copy(k):
            ref = at(y, z, 0, rows)
            target = lax.rem(z + order(NZ - 1 - k), NZ)
            return remote(ref, ref, gz_ss.at[p, k], gz_rs.at[p, k], to_z(target))

        def z_arrival(k):
            ref = at(y, zp_of(k), 0, rows)
            target = lax.rem(z + order(NZ - 1 - k), NZ)
            return remote(ref, ref, gz_ss.at[p, k], gz_rs.at[p, k], to_z(target))

        def b_send(k):
            ref = at(y, zp_of(k), 0, rows)
            return (
                remote(ref, ref, gb_ss.at[p, 0, k], gb_rs.at[p, 0, k], to_up),
                remote(ref, ref, gb_ss.at[p, 1, k], gb_rs.at[p, 1, k], to_dn),
            )

        def b_arrival(k):
            from_dn = at(y_dn, zp_of(k), 0, rows)
            from_up = at(y_up, zp_of(k), 0, rows)
            return (
                remote(from_dn, from_dn, gb_ss.at[p, 0, k], gb_rs.at[p, 0, k], to_up),
                remote(from_up, from_up, gb_ss.at[p, 1, k], gb_rs.at[p, 1, k], to_dn),
            )

        def a_send(k):
            up = at(y_dn, zp_of(k), 0, half)
            dn = at(y_up, zp_of(k), half, half)
            return (
                remote(up, up, ga_ss.at[p, 0, k], ga_rs.at[p, 0, k], to_up),
                remote(dn, dn, ga_ss.at[p, 1, k], ga_rs.at[p, 1, k], to_dn),
            )

        def a_arrival(k):
            first = at(y_far, zp_of(k), 0, half)
            second = at(y_far, zp_of(k), half, half)
            return (
                remote(first, first, ga_ss.at[p, 0, k], ga_rs.at[p, 0, k], to_up),
                remote(second, second, ga_ss.at[p, 1, k], ga_rs.at[p, 1, k], to_dn),
            )

        def first_leg(k, wait):
            if wait:
                z_arrival(k).wait_recv()
            for copy in b_send(k):
                copy.start()
            arrived(y, 0, zp_of(k), k)

        def second_leg(k):
            got = b_arrival(k)
            go = a_send(k)
            got[0].wait_recv()
            go[0].start()
            got[1].wait_recv()
            go[1].start()
            arrived(y_dn, 3, zp_of(k), k)
            arrived(y_up, 1, zp_of(k), k)

        def last_leg(k):
            for copy in a_arrival(k):
                copy.wait_recv()
            arrived(y_far, 2, zp_of(k), k)

        first_leg(0, False)
        for k in range(1, NZ):
            z_copy(k).start()
        start_more()

        def step(k, carry):
            first_leg(k, True)
            second_leg(k - 1)

            @pl.when(k >= 2)
            def _():
                last_leg(k - 2)

            @pl.when(k >= 3)
            def _():
                use(zp_of(k - 3), k - 3)

            return carry

        lax.fori_loop(1, NZ, step, 0)
        second_leg(NZ - 1)
        last_leg(NZ - 2)
        if NZ > 2:
            use(zp_of(NZ - 3), NZ - 3)
        use(zp_of(NZ - 2), NZ - 2)
        last_leg(NZ - 1)
        use(zp_of(NZ - 1), NZ - 1)

        def drain():
            def one(k, carry):
                for copy in b_send(k) + a_send(k):
                    copy.wait_send()

                @pl.when(k >= 1)
                def _():
                    z_copy(k).wait_send()

                return carry

            lax.fori_loop(0, NZ, one, 0)

        return drain

    def backward(acc, buf, t, zz):
        for ya, yb in ((y, y_dn), (y_up, y_far)):
            left = jnp.concatenate([buf[ya, zz], buf[yb, zz]], axis=1)
            row = pl.ds(pl.multiple_of(zz * W, W), W)
            right = jnp.concatenate([tiles[t, ya, row, :], tiles[t, yb, row, :]], axis=0)
            acc[...] += jnp.dot(left, right, preferred_element_type=F32)

    other = pl.ds(pl.multiple_of((1 - s) * W, W), W)

    def pair_copy(yy, o, zz, k):
        ref = top_all.at[yy, zz, mine]
        return remote(ref, ref, pair_ss.at[o, k], pair_rs.at[o, k], to_pair)

    def pair_arrival(yy, o, zz, k):
        ref = top_all.at[yy, zz, other]
        return remote(ref, ref, pair_ss.at[o, k], pair_rs.at[o, k], to_pair)

    def top_arrived(yy, o, zz, k):
        pair_copy(yy, o, zz, k).start()

    full_copy = remote(
        top_full.at[mine], top_full.at[mine], full_ss.at[0], full_rs.at[0], to_pair
    )

    def top_start():
        full_copy.start()
        acc_sep[...] = jnp.zeros_like(acc_sep)
        acc_leaf[...] = jnp.zeros_like(acc_leaf)
        drain_top()

    def top_use(zz, k):
        for o, yy in enumerate((y, y_up, y_far, y_dn)):
            pair_arrival(yy, o, zz, k).wait_recv()
        backward(acc_sep, top_all, 2, zz)

    drain_gtop = gather_col(0, top_all, s * W, W, top_start, top_arrived, top_use)

    def x_reduce(p, acc):
        def copy(o):
            return remote(
                xr_send.at[p, o], xr_recv.at[p, o], xr_ss.at[p, o], xr_rs.at[p, o], to_x(o)
            )

        for o in range(1, NX):
            lane = pl.ds(pl.multiple_of(lax.rem(x + o, NX) * W, W), W)
            xr_send[p, o] = acc[:, lane].astype(BF)
            copy(o).start()
        out = acc[:, pl.ds(pl.multiple_of(x * W, W), W)]
        for o in range(1, NX):
            copy(o).wait_recv()
            out = out + xr_recv[p, o].astype(F32)

        def drain():
            for o in range(1, NX):
                copy(o).wait_send()

        return out, drain

    sep_t, drain_x0 = x_reduce(0, acc_sep)
    sx = jnp.dot(sep_y[...].T - sep_t, sep_inv[...], precision=HI, preferred_element_type=F32)
    sepx_all[y, z] = sx.astype(BF)

    def sep_start():
        sep_out[...] = sx
        drain_x0()
        drain_gtop()

        def one(k, carry):
            zz = lax.rem(z + NZ - order(NZ - 1 - k), NZ)
            for o, yy in enumerate((y, y_up, y_far, y_dn)):
                pair_copy(yy, o, zz, k).wait_send()
            return carry

        lax.fori_loop(0, NZ, one, 0)
        full_copy.wait()
        top_out[...] = top_full[...]

    def sep_use(zz, k):
        backward(acc_leaf, top_all, 1, zz)
        backward(acc_leaf, sepx_all, 0, zz)

    drain_gsep = gather_col(
        1, sepx_all, 0, 2 * W, sep_start, lambda yy, o, zz, k: None, sep_use
    )
    leaf_t, drain_x1 = x_reduce(1, acc_leaf)
    leaf_out[...] = jnp.dot(
        leaf_y[...].T - leaf_t, leaf_inv[...], precision=HI, preferred_element_type=F32
    )
    drain_gsep()
    drain_x1()


def body(
    leaf_rhs,
    sep_rhs,
    top_rhs,
    leaf_inv,
    sep_inv,
    top_inv,
    sep_leaf,
    top_leaf,
    top_sep,
    sep_leaf_mask,
    top_leaf_mask,
    top_sep_mask,
):
    W = 128
    R = leaf_rhs.shape[-1]
    NC = sep_leaf.shape[2]
    NX = sep_leaf.shape[4]
    NZ = NC // NY
    rows = NC * W * NX

    def pattern(mask):
        return mask.reshape(NC, NX).T.reshape(NX, 1, NC)

    vm = pl.BlockSpec(memory_space=pltpu.VMEM)
    sm = pl.BlockSpec(memory_space=pltpu.SMEM)
    hbm = pl.BlockSpec(memory_space=pl.ANY)
    dma = pltpu.SemaphoreType.DMA
    out = jax.ShapeDtypeStruct((R, W), F32)
    H = W // 2

    def stage(cols):
        return [
            pltpu.VMEM((NZ, W, cols), BF),
            pltpu.VMEM((2, NZ, H, cols), BF),
            pltpu.VMEM((2, NZ, W, cols), BF),
            pltpu.VMEM((2, NZ, W, cols), BF),
            pltpu.VMEM((NZ, W, cols), BF),
            pltpu.VMEM((NZ, W, cols), BF),
        ]

    scratch = (
        [
            pltpu.VMEM((3, rows, W), BF),
            pltpu.VMEM((3, NY, NZ * W, NX * W), BF),
            pltpu.VMEM((64 * NX, 64 * NX), BF),
            pltpu.VMEM((W, R), F32),
            pltpu.VMEM((W, R), F32),
            pltpu.VMEM((NX, W, R), BF),
            pltpu.VMEM((NX, W, R), BF),
            pltpu.VMEM((NY, NZ * W, R), F32),
            pltpu.VMEM((2, NY, NZ * W, W), F32),
            pltpu.VMEM((NY, NZ * W, W), BF),
            pltpu.VMEM((NY, NZ * W, W), BF),
        ]
        + stage(R)
        + stage(W)
        + [
            pltpu.VMEM((R, W), F32),
            pltpu.VMEM((NY, NZ, R, W), BF),
            pltpu.VMEM((NY, NZ, R, W), BF),
            pltpu.VMEM((R, NX * W), F32),
            pltpu.VMEM((R, NX * W), F32),
            pltpu.VMEM((2, NX, R, W), BF),
            pltpu.VMEM((2, NX, R, W), BF),
            dma((3,)),
        ]
        + [dma((2, NX))] * 4
        + [dma((2, 2, NZ))] * 4
        + [dma((2, NZ))] * 2
        + [dma((NY,))] * 2
        + [dma((2, 2, NZ))] * 4
        + [dma((2, NZ))] * 2
        + [dma((NY, NZ))] * 2
        + [dma((1,))] * 2
    )
    lx, sx, tx = pl.pallas_call(
        functools.partial(kernel, NX, NZ),
        out_shape=(out, out, out),
        in_specs=[vm] * 6 + [hbm] * 3 + [sm] * 3,
        out_specs=(vm, vm, vm),
        scratch_shapes=scratch,
        compiler_params=pltpu.CompilerParams(
            collective_id=0, has_side_effects=True, vmem_limit_bytes=62 * 1024 * 1024
        ),
    )(
        leaf_rhs.reshape(W, R),
        sep_rhs.reshape(W, R),
        top_rhs.reshape(W, R),
        leaf_inv.reshape(W, W),
        sep_inv.reshape(W, W),
        top_inv.reshape(W, W),
        sep_leaf.reshape(rows, W),
        top_leaf.reshape(rows, W),
        top_sep.reshape(rows, W),
        pattern(sep_leaf_mask),
        pattern(top_leaf_mask),
        pattern(top_sep_mask),
    )
    return (lx.T[None, None, None, None], sx.T[None, None, None], tx.T[None, None])


def solution(mesh):
    in_specs = (
        P("sec", "row", None, "col", None, None),
        P("sec", "row", "col", None, None),
        P("row", "col", None, None),
        P("sec", "row", None, "col", None, None),
        P("sec", "row", "col", None, None),
        P("row", "col", None, None),
        P("sec", "row", None, None, None, None, "col", None),
        P("sec", "row", None, None, None, None, "col", None),
        P("sec", "row", None, None, None, "col", None),
        P("sec", "row", None, None, None, "col"),
        P("sec", "row", None, None, None, "col"),
        P("sec", "row", None, None, "col"),
    )
    out_specs = (
        P("sec", "row", None, "col", None, None),
        P("sec", "row", "col", None, None),
        P("row", "col", None, None),
    )
    return jax.shard_map(body, mesh=mesh, in_specs=in_specs, out_specs=out_specs, check_vma=False)
```

```python
import functools

import jax
import jax.numpy as jnp
from jax import lax
from jax.experimental import pallas as pl
from jax.experimental.pallas import tpu as pltpu
from jax.sharding import PartitionSpec as P

MESH = pl.DeviceIdType.MESH
NY = 4
BF = jnp.bfloat16
F32 = jnp.float32
HI = lax.Precision.HIGHEST


def kernel(
    NX,
    NZ,
    leaf_rhs_hbm,
    sep_rhs_hbm,
    top_rhs_hbm,
    leaf_inv_hbm,
    sep_inv_hbm,
    top_inv_hbm,
    sl_hbm,
    tl_hbm,
    ts_hbm,
    sl_mask_hbm,
    tl_mask_hbm,
    ts_mask_hbm,
    leaf_out,
    sep_out,
    top_out,
    leaf_rhs,
    sep_rhs,
    top_rhs,
    leaf_inv,
    sep_inv,
    top_inv,
    sl_mask,
    tl_mask,
    ts_mask,
    raw,
    tiles,
    select,
    leaf_y,
    sep_y,
    leaf_all,
    sep_all,
    part,
    top_part,
    swap_out,
    swap_in,
    fa_send,
    fa_recv,
    fb_send,
    fb_recv,
    fz_send,
    fz_recv,
    ta_send,
    ta_recv,
    tb_send,
    tb_recv,
    tz_send,
    tz_recv,
    top_full,
    top_all,
    sepx_all,
    acc_sep,
    acc_leaf,
    xr_send,
    xr_recv,
    load_sem,
    small_sem,
    xg_ss,
    xg_rs,
    xr_ss,
    xr_rs,
    a_ss,
    a_rs,
    b_ss,
    b_rs,
    z_ss,
    z_rs,
    swap_ss,
    swap_rs,
    ga_ss,
    ga_rs,
    gb_ss,
    gb_rs,
    gz_ss,
    gz_rs,
    pair_ss,
    pair_rs,
    full_ss,
    full_rs,
):
    W = 128
    NC = NY * NZ
    s = lax.axis_index("sec")
    x = lax.axis_index("row")
    c = lax.axis_index("col")
    z = c // NY
    y = c % NY

    def col_of(yy, zz):
        return zz * NY + yy

    y_up = lax.rem(y + 1, NY)
    y_far = lax.rem(y + 2, NY)
    y_dn = lax.rem(y + 3, NY)
    to_up = (s, x, col_of(y_up, z))
    to_dn = (s, x, col_of(y_dn, z))
    to_pair = (1 - s, x, c)

    def to_x(o):
        return (s, lax.rem(x + o, NX), c)

    def to_z(zz):
        return (s, x, col_of(y, zz))

    def order(k):
        half = (k + 1) // 2
        return NZ // 2 + half * (1 - 2 * lax.rem(k, 2))

    def remote(src, dst, ss, rs, dev):
        return pltpu.make_async_remote_copy(
            src_ref=src,
            dst_ref=dst,
            send_sem=ss,
            recv_sem=rs,
            device_id=dev,
            device_id_type=MESH,
        )

    loads = [
        pltpu.make_async_copy(ref, raw.at[t], load_sem.at[t])
        for t, ref in enumerate((sl_hbm, tl_hbm, ts_hbm))
    ]
    small = [
        pltpu.make_async_copy(src, dst, small_sem.at[i])
        for i, (src, dst) in enumerate(
            (
                (leaf_rhs_hbm, leaf_rhs),
                (leaf_inv_hbm, leaf_inv),
                (sl_mask_hbm, sl_mask),
                (sep_rhs_hbm, sep_rhs),
                (sep_inv_hbm, sep_inv),
                (top_rhs_hbm, top_rhs),
                (top_inv_hbm, top_inv),
                (tl_mask_hbm, tl_mask),
                (ts_mask_hbm, ts_mask),
            )
        )
    ]
    for load in small[0:3]:
        load.start()
    loads[0].start()
    for load in small[3:]:
        load.start()

    barrier = pltpu.get_barrier_semaphore()

    def greet(dev):
        pl.semaphore_signal(barrier, inc=1, device_id=dev, device_id_type=MESH)

    greet(to_pair)
    for o in range(1, NX):
        greet(to_x(o))
    greet(to_up)
    greet(to_dn)
    for o in range(1, NZ):
        greet(to_z(lax.rem(z + o, NZ)))

    small[0].wait()
    small[1].wait()
    ly = jnp.dot(leaf_inv[...], leaf_rhs[...].astype(F32), precision=HI, preferred_element_type=F32)
    leaf_y[...] = ly
    leaf_all[x] = ly.astype(BF)

    pl.semaphore_wait(barrier, NX + NZ + 1)

    def x_gather(p, buf):
        return [
            remote(buf.at[x], buf.at[x], xg_ss.at[p, o], xg_rs.at[p, o], to_x(o))
            for o in range(1, NX)
        ]

    leaf_sends = x_gather(0, leaf_all)
    for copy in leaf_sends:
        copy.start()

    SB = 64
    rows_i = lax.broadcasted_iota(jnp.int32, (SB * NX, SB * NX), 0)
    cols_i = lax.broadcasted_iota(jnp.int32, (SB * NX, SB * NX), 1)
    wanted = lax.rem(rows_i, SB) * NX + rows_i // SB
    select[...] = jnp.where(cols_i == wanted, 1.0, 0.0).astype(BF)

    def prep(t, mask, lo, n):
        def unit(i, carry):
            cc = lo + i
            yy = lax.rem(cc, NY)
            zz = cc // NY
            start = pl.multiple_of(cc * (W * NX), W * NX)
            block = jnp.concatenate(
                [raw[t, pl.ds(start + sub * (SB * NX), SB * NX), :] for sub in range(W // SB)],
                axis=1,
            )
            moved = jnp.dot(select[...], block, preferred_element_type=F32)
            for r in range(NX):
                keep = mask[r, 0, cc].astype(F32)
                for sub in range(W // SB):
                    row = pl.multiple_of(zz * W + sub * SB, SB)
                    tiles[t, yy, pl.ds(row, SB), r * W : (r + 1) * W] = (
                        moved[r * SB : (r + 1) * SB, sub * W : (sub + 1) * W] * keep
                    ).astype(BF)
            return carry

        lax.fori_loop(0, n, unit, 0)

    for load in small[2:]:
        load.wait()
    loads[0].wait()
    loads[1].start()
    loads[2].start()
    prep(0, sl_mask, 0, NC)

    for copy in leaf_sends:
        copy.wait()

    MB = min(512, NZ * W)

    def forward(t, values, yy, write):
        def block(i, carry):
            row = pl.multiple_of(i * MB, MB)
            out = jnp.dot(
                tiles[t, yy, pl.ds(row, MB), :],
                values[...].reshape(NX * W, 2 * W),
                preferred_element_type=F32,
            )
            write(row, out)
            return carry

        lax.fori_loop(0, NZ * W // MB, block, 0)

    def sep_dot(yy):
        def write(row, out):
            part[yy, pl.ds(row, MB), :] = out

        forward(0, leaf_all, yy, write)

    H = W // 2

    def reduce_col(p, chunk, start_more, work, a_s, a_r, b_s, b_r, z_s, z_r):
        def zp_of(k):
            return lax.rem(z + order(k), NZ)

        def a_copies(k):
            return (
                remote(a_s.at[k, 0:H], a_r.at[0, k], a_ss.at[p, 0, k], a_rs.at[p, 0, k], to_up),
                remote(a_s.at[k, H:W], a_r.at[1, k], a_ss.at[p, 1, k], a_rs.at[p, 1, k], to_dn),
            )

        def b_copies(k):
            return (
                remote(b_s.at[0, k], b_r.at[0, k], b_ss.at[p, 0, k], b_rs.at[p, 0, k], to_up),
                remote(b_s.at[1, k], b_r.at[1, k], b_ss.at[p, 1, k], b_rs.at[p, 1, k], to_dn),
            )

        def z_copy(k):
            return remote(z_s.at[k], z_r.at[k], z_ss.at[p, k], z_rs.at[p, k], to_z(zp_of(k)))

        def send_a(k):
            a_s[k] = chunk(y_far, zp_of(k), 0, W).astype(BF)
            for copy in a_copies(k):
                copy.start()

        def send_b(k):
            zp = zp_of(k)
            up, dn = a_copies(k)
            cup, cdn = b_copies(k)
            b_s[0, k, H:W] = chunk(y_up, zp, H, H).astype(BF)
            b_s[1, k, 0:H] = chunk(y_dn, zp, 0, H).astype(BF)
            up.wait_recv()
            b_s[0, k, 0:H] = (chunk(y_up, zp, 0, H) + a_r[0, k].astype(F32)).astype(BF)
            cup.start()
            dn.wait_recv()
            b_s[1, k, H:W] = (chunk(y_dn, zp, H, H) + a_r[1, k].astype(F32)).astype(BF)
            cdn.start()

        def total(k):
            for copy in b_copies(k):
                copy.wait_recv()
            return chunk(y, zp_of(k), 0, W) + b_r[0, k].astype(F32) + b_r[1, k].astype(F32)

        def send_z(k):
            z_s[k] = total(k).astype(BF)
            z_copy(k).start()

        ahead = min(3, NZ)
        for k in range(ahead):
            send_a(k)
        start_more()

        def step(k, carry):
            @pl.when(k < NZ - ahead)
            def _():
                send_a(k + ahead)

            send_b(k)
            work(k)

            @pl.when(k >= 2)
            def _():
                send_z(k - 2)

            return carry

        lax.fori_loop(0, NZ, step, 0)
        send_z(NZ - 2)
        out = total(NZ - 1)
        for k in range(NZ - 1):
            z_copy(k).wait_recv()
            out = out + z_r[k].astype(F32)

        def drain():
            def one(k, carry):
                for copy in a_copies(k) + b_copies(k):
                    copy.wait_send()

                @pl.when(k < NZ - 1)
                def _():
                    z_copy(k).wait_send()

                return carry

            lax.fori_loop(0, NZ, one, 0)

        return out, drain

    sep_dot(y_far)

    def sep_more():
        sep_dot(y_up)
        sep_dot(y_dn)
        sep_dot(y)

    def sep_chunk(yy, zp, lo, n):
        return part[yy, pl.ds(pl.multiple_of(zp * W + lo, n), n), :]

    per = max(1, 2 * NC // NZ)
    split = NZ // 2

    def top_leaf_dot(yy):
        def write(row, out):
            top_part[0, yy, pl.ds(row, MB), :] = out[:, 0:W]
            top_part[1, yy, pl.ds(row, MB), :] = out[:, W : 2 * W]

        forward(1, leaf_all, yy, write)

    def sep_work(k):
        @pl.when(k == 0)
        def _():
            loads[1].wait()
            loads[2].wait()

        @pl.when(k < split)
        def _():
            prep(1, tl_mask, k * per, per)

        @pl.when(k >= split)
        def _():
            prep(2, ts_mask, (k - split) * per, per)

        @pl.when(k == split)
        def _():
            top_leaf_dot(y)
            top_leaf_dot(y_up)

        @pl.when(k == NZ - 1)
        def _():
            top_leaf_dot(y_dn)
            top_leaf_dot(y_far)

    sep_sum, drain_sep = reduce_col(
        0, sep_chunk, sep_more, sep_work, fa_send, fa_recv, fb_send, fb_recv, fz_send, fz_recv
    )
    sy = jnp.dot(
        sep_inv[...],
        sep_rhs[...].astype(F32) - sep_sum,
        precision=HI,
        preferred_element_type=F32,
    )
    sep_y[...] = sy
    sep_all[x] = sy.astype(BF)
    sep_sends = x_gather(1, sep_all)
    for copy in sep_sends:
        copy.start()
    drain_sep()
    for copy in sep_sends:
        copy.wait()

    order_y = (y_far, y_up, y_dn, y)

    def swap_copy(i):
        return remote(
            swap_out.at[i], swap_in.at[i], swap_ss.at[i], swap_rs.at[i], to_pair
        )

    for i, yy in enumerate(order_y):

        def write(row, out, i=i, yy=yy):
            top_part[0, yy, pl.ds(row, MB), :] += out[:, 0:W]
            top_part[1, yy, pl.ds(row, MB), :] += out[:, W : 2 * W]
            swap_out[i, pl.ds(row, MB), :] = top_part[1 - s, yy, pl.ds(row, MB), :].astype(BF)

        forward(2, sep_all, yy, write)
        swap_copy(i).start()

    def join(i, yy):
        swap_copy(i).wait()

        def block(j, carry):
            row = pl.multiple_of(j * W, W)
            top_part[s, yy, pl.ds(row, W), :] += swap_in[i, pl.ds(row, W), :].astype(F32)
            return carry

        lax.fori_loop(0, NZ, block, 0)

    join(0, y_far)

    def top_more():
        join(1, y_up)
        join(2, y_dn)
        join(3, y)

    def top_chunk(yy, zp, lo, n):
        return top_part[s, yy, pl.ds(pl.multiple_of(zp * W + lo, n), n), :]

    top_sum, drain_top = reduce_col(
        1, top_chunk, top_more, lambda k: None, ta_send, ta_recv, tb_send, tb_recv, tz_send, tz_recv
    )
    mine = pl.ds(pl.multiple_of(s * W, W), W)
    ty = jnp.dot(
        top_inv[...],
        top_rhs[:, mine].astype(F32) - top_sum,
        precision=HI,
        preferred_element_type=F32,
    )
    tx = jnp.dot(ty.T, top_inv[...], precision=HI, preferred_element_type=F32)
    top_full[mine, :] = tx
    top_all[y, z, mine, :] = tx.astype(BF)

    def gather_col(p, buf, lo, rows, start_more, arrived, use):
        def zp_of(k):
            return lax.rem(z + NZ - order(NZ - 1 - k), NZ)

        def at(yy, zz, first, n):
            return buf.at[yy, zz, pl.ds(pl.multiple_of(lo + first, n), n)]

        half = rows // 2

        def z_copy(k):
            ref = at(y, z, 0, rows)
            target = lax.rem(z + order(NZ - 1 - k), NZ)
            return remote(ref, ref, gz_ss.at[p, k], gz_rs.at[p, k], to_z(target))

        def z_arrival(k):
            ref = at(y, zp_of(k), 0, rows)
            target = lax.rem(z + order(NZ - 1 - k), NZ)
            return remote(ref, ref, gz_ss.at[p, k], gz_rs.at[p, k], to_z(target))

        def b_send(k):
            ref = at(y, zp_of(k), 0, rows)
            return (
                remote(ref, ref, gb_ss.at[p, 0, k], gb_rs.at[p, 0, k], to_up),
                remote(ref, ref, gb_ss.at[p, 1, k], gb_rs.at[p, 1, k], to_dn),
            )

        def b_arrival(k):
            from_dn = at(y_dn, zp_of(k), 0, rows)
            from_up = at(y_up, zp_of(k), 0, rows)
            return (
                remote(from_dn, from_dn, gb_ss.at[p, 0, k], gb_rs.at[p, 0, k], to_up),
                remote(from_up, from_up, gb_ss.at[p, 1, k], gb_rs.at[p, 1, k], to_dn),
            )

        def a_send(k):
            up = at(y_dn, zp_of(k), 0, half)
            dn = at(y_up, zp_of(k), half, half)
            return (
                remote(up, up, ga_ss.at[p, 0, k], ga_rs.at[p, 0, k], to_up),
                remote(dn, dn, ga_ss.at[p, 1, k], ga_rs.at[p, 1, k], to_dn),
            )

        def a_arrival(k):
            first = at(y_far, zp_of(k), 0, half)
            second = at(y_far, zp_of(k), half, half)
            return (
                remote(first, first, ga_ss.at[p, 0, k], ga_rs.at[p, 0, k], to_up),
                remote(second, second, ga_ss.at[p, 1, k], ga_rs.at[p, 1, k], to_dn),
            )

        def first_leg(k, wait):
            if wait:
                z_arrival(k).wait_recv()
            for copy in b_send(k):
                copy.start()
            arrived(y, 0, zp_of(k), k)

        def second_leg(k):
            got = b_arrival(k)
            go = a_send(k)
            got[0].wait_recv()
            go[0].start()
            got[1].wait_recv()
            go[1].start()
            arrived(y_dn, 3, zp_of(k), k)
            arrived(y_up, 1, zp_of(k), k)

        def last_leg(k):
            for copy in a_arrival(k):
                copy.wait_recv()
            arrived(y_far, 2, zp_of(k), k)

        first_leg(0, False)
        for k in range(1, NZ):
            z_copy(k).start()
        start_more()

        behind = min(2, NZ - 1)

        def step(k, carry):
            first_leg(k, True)

            @pl.when(k >= behind)
            def _():
                second_leg(k - behind)

            return carry

        lax.fori_loop(1, NZ, step, 0)
        for k in range(NZ - behind, NZ):
            second_leg(k)

        def finish(k, carry):
            last_leg(k)

            @pl.when(k >= 1)
            def _():
                use(zp_of(k - 1), k - 1)

            return carry

        lax.fori_loop(0, NZ, finish, 0)
        use(zp_of(NZ - 1), NZ - 1)

        def drain():
            def one(k, carry):
                for copy in b_send(k) + a_send(k):
                    copy.wait_send()

                @pl.when(k >= 1)
                def _():
                    z_copy(k).wait_send()

                return carry

            lax.fori_loop(0, NZ, one, 0)

        return drain

    def backward(acc, buf, t, zz):
        for ya, yb in ((y, y_dn), (y_up, y_far)):
            left = jnp.concatenate([buf[ya, zz], buf[yb, zz]], axis=1)
            row = pl.ds(pl.multiple_of(zz * W, W), W)
            right = jnp.concatenate([tiles[t, ya, row, :], tiles[t, yb, row, :]], axis=0)
            acc[...] += jnp.dot(left, right, preferred_element_type=F32)

    other = pl.ds(pl.multiple_of((1 - s) * W, W), W)

    def pair_copy(yy, o, zz, k):
        ref = top_all.at[yy, zz, mine]
        return remote(ref, ref, pair_ss.at[o, k], pair_rs.at[o, k], to_pair)

    def pair_arrival(yy, o, zz, k):
        ref = top_all.at[yy, zz, other]
        return remote(ref, ref, pair_ss.at[o, k], pair_rs.at[o, k], to_pair)

    def top_arrived(yy, o, zz, k):
        pair_copy(yy, o, zz, k).start()

    full_copy = remote(
        top_full.at[mine], top_full.at[mine], full_ss.at[0], full_rs.at[0], to_pair
    )

    def top_start():
        full_copy.start()
        acc_sep[...] = jnp.zeros_like(acc_sep)
        acc_leaf[...] = jnp.zeros_like(acc_leaf)
        drain_top()

    def top_use(zz, k):
        for o, yy in enumerate((y, y_up, y_far, y_dn)):
            pair_arrival(yy, o, zz, k).wait_recv()
        backward(acc_sep, top_all, 2, zz)

    drain_gtop = gather_col(0, top_all, s * W, W, top_start, top_arrived, top_use)

    def x_reduce(p, acc):
        def copy(o):
            return remote(
                xr_send.at[p, o], xr_recv.at[p, o], xr_ss.at[p, o], xr_rs.at[p, o], to_x(o)
            )

        for o in range(1, NX):
            lane = pl.ds(pl.multiple_of(lax.rem(x + o, NX) * W, W), W)
            xr_send[p, o] = acc[:, lane].astype(BF)
            copy(o).start()
        out = acc[:, pl.ds(pl.multiple_of(x * W, W), W)]
        for o in range(1, NX):
            copy(o).wait_recv()
            out = out + xr_recv[p, o].astype(F32)

        def drain():
            for o in range(1, NX):
                copy(o).wait_send()

        return out, drain

    sep_t, drain_x0 = x_reduce(0, acc_sep)
    sx = jnp.dot(sep_y[...].T - sep_t, sep_inv[...], precision=HI, preferred_element_type=F32)
    sepx_all[y, z] = sx.astype(BF)

    def sep_start():
        sep_out[...] = sx
        drain_x0()
        drain_gtop()

        def one(k, carry):
            zz = lax.rem(z + NZ - order(NZ - 1 - k), NZ)
            for o, yy in enumerate((y, y_up, y_far, y_dn)):
                pair_copy(yy, o, zz, k).wait_send()
            return carry

        lax.fori_loop(0, NZ, one, 0)
        full_copy.wait()
        top_out[...] = top_full[...]

    def sep_use(zz, k):
        backward(acc_leaf, top_all, 1, zz)
        backward(acc_leaf, sepx_all, 0, zz)

    drain_gsep = gather_col(
        1, sepx_all, 0, 2 * W, sep_start, lambda yy, o, zz, k: None, sep_use
    )
    leaf_t, drain_x1 = x_reduce(1, acc_leaf)
    leaf_out[...] = jnp.dot(
        leaf_y[...].T - leaf_t, leaf_inv[...], precision=HI, preferred_element_type=F32
    )
    drain_gsep()
    drain_x1()


def body(
    leaf_rhs,
    sep_rhs,
    top_rhs,
    leaf_inv,
    sep_inv,
    top_inv,
    sep_leaf,
    top_leaf,
    top_sep,
    sep_leaf_mask,
    top_leaf_mask,
    top_sep_mask,
):
    W = 128
    R = leaf_rhs.shape[-1]
    NC = sep_leaf.shape[2]
    NX = sep_leaf.shape[4]
    NZ = NC // NY
    rows = NC * W * NX

    def pattern(mask):
        return mask.reshape(NC, NX).T.reshape(NX, 1, NC)

    vm = pl.BlockSpec(memory_space=pltpu.VMEM)
    hbm = pl.BlockSpec(memory_space=pltpu.HBM)
    dma = pltpu.SemaphoreType.DMA
    out = jax.ShapeDtypeStruct((R, W), F32)
    H = W // 2

    def stage(cols):
        return [
            pltpu.VMEM((NZ, W, cols), BF),
            pltpu.VMEM((2, NZ, H, cols), BF),
            pltpu.VMEM((2, NZ, W, cols), BF),
            pltpu.VMEM((2, NZ, W, cols), BF),
            pltpu.VMEM((NZ, W, cols), BF),
            pltpu.VMEM((NZ, W, cols), BF),
        ]

    scratch = (
        [pltpu.VMEM((W, R), BF)] * 3
        + [pltpu.VMEM((W, W), F32)] * 3
        + [pltpu.SMEM((NX, 1, NC), jnp.int32)] * 3
        + [
            pltpu.VMEM((3, rows, W), BF),
            pltpu.VMEM((3, NY, NZ * W, NX * W), BF),
            pltpu.VMEM((64 * NX, 64 * NX), BF),
            pltpu.VMEM((W, R), F32),
            pltpu.VMEM((W, R), F32),
            pltpu.VMEM((NX, W, R), BF),
            pltpu.VMEM((NX, W, R), BF),
            pltpu.VMEM((NY, NZ * W, R), F32),
            pltpu.VMEM((2, NY, NZ * W, W), F32),
            pltpu.VMEM((NY, NZ * W, W), BF),
            pltpu.VMEM((NY, NZ * W, W), BF),
        ]
        + stage(R)
        + stage(W)
        + [
            pltpu.VMEM((R, W), F32),
            pltpu.VMEM((NY, NZ, R, W), BF),
            pltpu.VMEM((NY, NZ, R, W), BF),
            pltpu.VMEM((R, NX * W), F32),
            pltpu.VMEM((R, NX * W), F32),
            pltpu.VMEM((2, NX, R, W), BF),
            pltpu.VMEM((2, NX, R, W), BF),
            dma((3,)),
            dma((9,)),
        ]
        + [dma((2, NX))] * 4
        + [dma((2, 2, NZ))] * 4
        + [dma((2, NZ))] * 2
        + [dma((NY,))] * 2
        + [dma((2, 2, NZ))] * 4
        + [dma((2, NZ))] * 2
        + [dma((NY, NZ))] * 2
        + [dma((1,))] * 2
    )
    lx, sx, tx = pl.pallas_call(
        functools.partial(kernel, NX, NZ),
        out_shape=(out, out, out),
        in_specs=[hbm] * 12,
        out_specs=(vm, vm, vm),
        scratch_shapes=scratch,
        compiler_params=pltpu.CompilerParams(
            collective_id=0, has_side_effects=True, vmem_limit_bytes=50 * 1024 * 1024
        ),
    )(
        *(
            pltpu.with_memory_space_constraint(v, pltpu.HBM)
            for v in (
        leaf_rhs.reshape(W, R),
        sep_rhs.reshape(W, R),
        top_rhs.reshape(W, R),
        leaf_inv.reshape(W, W),
        sep_inv.reshape(W, W),
        top_inv.reshape(W, W),
        sep_leaf.reshape(rows, W),
        top_leaf.reshape(rows, W),
        top_sep.reshape(rows, W),
        pattern(sep_leaf_mask),
        pattern(top_leaf_mask),
        pattern(top_sep_mask),
            )
        )
    )
    return (lx.T[None, None, None, None], sx.T[None, None, None], tx.T[None, None])


def solution(mesh):
    in_specs = (
        P("sec", "row", None, "col", None, None),
        P("sec", "row", "col", None, None),
        P("row", "col", None, None),
        P("sec", "row", None, "col", None, None),
        P("sec", "row", "col", None, None),
        P("row", "col", None, None),
        P("sec", "row", None, None, None, None, "col", None),
        P("sec", "row", None, None, None, None, "col", None),
        P("sec", "row", None, None, None, "col", None),
        P("sec", "row", None, None, None, "col"),
        P("sec", "row", None, None, None, "col"),
        P("sec", "row", None, None, "col"),
    )
    out_specs = (
        P("sec", "row", None, "col", None, None),
        P("sec", "row", "col", None, None),
        P("row", "col", None, None),
    )
    return jax.shard_map(body, mesh=mesh, in_specs=in_specs, out_specs=out_specs, check_vma=False)
```

```python
import functools

import jax
import jax.numpy as jnp
from jax import lax
from jax.experimental import pallas as pl
from jax.experimental.pallas import tpu as pltpu
from jax.sharding import PartitionSpec as P

MESH = pl.DeviceIdType.MESH
NY = 4
BF = jnp.bfloat16
F32 = jnp.float32
HI = lax.Precision.HIGHEST


def kernel(
    NX,
    NZ,
    leaf_rhs_hbm,
    sep_rhs_hbm,
    top_rhs_hbm,
    leaf_inv_hbm,
    sep_inv_hbm,
    top_inv_hbm,
    sl_hbm,
    tl_hbm,
    ts_hbm,
    sl_mask_hbm,
    tl_mask_hbm,
    ts_mask_hbm,
    leaf_out,
    sep_out,
    top_out,
    leaf_rhs,
    sep_rhs,
    top_rhs,
    leaf_inv,
    sep_inv,
    top_inv,
    sl_mask,
    tl_mask,
    ts_mask,
    raw,
    tiles,
    select,
    leaf_y,
    sep_y,
    leaf_all,
    sep_all,
    part,
    top_part,
    swap_out,
    swap_in,
    fa_send,
    fa_recv,
    fb_send,
    fb_recv,
    fz_send,
    fz_recv,
    ta_send,
    ta_recv,
    tb_send,
    tb_recv,
    tz_send,
    tz_recv,
    top_full,
    top_all,
    sepx_all,
    acc_sep,
    acc_leaf,
    xr_send,
    xr_recv,
    load_sem,
    small_sem,
    xg_ss,
    xg_rs,
    xr_ss,
    xr_rs,
    a_ss,
    a_rs,
    b_ss,
    b_rs,
    z_ss,
    z_rs,
    swap_ss,
    swap_rs,
    ga_ss,
    ga_rs,
    gb_ss,
    gb_rs,
    gz_ss,
    gz_rs,
    pair_ss,
    pair_rs,
    full_ss,
    full_rs,
):
    W = 128
    NC = NY * NZ
    s = lax.axis_index("sec")
    x = lax.axis_index("row")
    c = lax.axis_index("col")
    z = c // NY
    y = c % NY

    def col_of(yy, zz):
        return zz * NY + yy

    y_up = lax.rem(y + 1, NY)
    y_far = lax.rem(y + 2, NY)
    y_dn = lax.rem(y + 3, NY)
    to_up = (s, x, col_of(y_up, z))
    to_dn = (s, x, col_of(y_dn, z))
    to_far = (s, x, col_of(y_far, z))
    to_pair = (1 - s, x, c)

    def to_x(o):
        return (s, lax.rem(x + o, NX), c)

    def to_z(zz):
        return (s, x, col_of(y, zz))

    def order(k):
        half = (k + 1) // 2
        return NZ // 2 + half * (1 - 2 * lax.rem(k, 2))

    def remote(src, dst, ss, rs, dev):
        return pltpu.make_async_remote_copy(
            src_ref=src,
            dst_ref=dst,
            send_sem=ss,
            recv_sem=rs,
            device_id=dev,
            device_id_type=MESH,
        )

    loads = [
        pltpu.make_async_copy(ref, raw.at[t], load_sem.at[t])
        for t, ref in enumerate((sl_hbm, tl_hbm, ts_hbm))
    ]
    small = [
        pltpu.make_async_copy(src, dst, small_sem.at[i])
        for i, (src, dst) in enumerate(
            (
                (leaf_rhs_hbm, leaf_rhs),
                (leaf_inv_hbm, leaf_inv),
                (sl_mask_hbm, sl_mask),
                (sep_rhs_hbm, sep_rhs),
                (sep_inv_hbm, sep_inv),
                (top_rhs_hbm, top_rhs),
                (top_inv_hbm, top_inv),
                (tl_mask_hbm, tl_mask),
                (ts_mask_hbm, ts_mask),
            )
        )
    ]
    for load in small[0:3]:
        load.start()
    loads[0].start()
    for load in small[3:]:
        load.start()

    barrier = pltpu.get_barrier_semaphore()

    def greet(dev):
        pl.semaphore_signal(barrier, inc=1, device_id=dev, device_id_type=MESH)

    greet(to_pair)
    for o in range(1, NX):
        greet(to_x(o))
    greet(to_up)
    greet(to_dn)
    greet(to_far)
    for o in range(1, NZ):
        greet(to_z(lax.rem(z + o, NZ)))

    small[0].wait()
    small[1].wait()
    ly = jnp.dot(leaf_inv[...], leaf_rhs[...].astype(F32), precision=HI, preferred_element_type=F32)
    leaf_y[...] = ly
    leaf_all[x] = ly.astype(BF)

    pl.semaphore_wait(barrier, NX + NZ + 2)

    def x_gather(p, buf):
        return [
            remote(buf.at[x], buf.at[x], xg_ss.at[p, o], xg_rs.at[p, o], to_x(o))
            for o in range(1, NX)
        ]

    leaf_sends = x_gather(0, leaf_all)
    for copy in leaf_sends:
        copy.start()

    SB = 64
    rows_i = lax.broadcasted_iota(jnp.int32, (SB * NX, SB * NX), 0)
    cols_i = lax.broadcasted_iota(jnp.int32, (SB * NX, SB * NX), 1)
    wanted = lax.rem(rows_i, SB) * NX + rows_i // SB
    select[...] = jnp.where(cols_i == wanted, 1.0, 0.0).astype(BF)

    def prep(t, mask, lo, n):
        def unit(i, carry):
            cc = lo + i
            yy = lax.rem(cc, NY)
            zz = cc // NY
            start = pl.multiple_of(cc * (W * NX), W * NX)
            block = jnp.concatenate(
                [raw[t, pl.ds(start + sub * (SB * NX), SB * NX), :] for sub in range(W // SB)],
                axis=1,
            )
            moved = jnp.dot(select[...], block, preferred_element_type=F32)
            for r in range(NX):
                keep = mask[r, 0, cc].astype(F32)
                for sub in range(W // SB):
                    row = pl.multiple_of(zz * W + sub * SB, SB)
                    tiles[t, yy, pl.ds(row, SB), r * W : (r + 1) * W] = (
                        moved[r * SB : (r + 1) * SB, sub * W : (sub + 1) * W] * keep
                    ).astype(BF)
            return carry

        lax.fori_loop(0, n, unit, 0)

    for load in small[2:]:
        load.wait()
    loads[0].wait()
    loads[1].start()
    loads[2].start()
    prep(0, sl_mask, 0, NC)

    for copy in leaf_sends:
        copy.wait()

    MB = min(512, NZ * W)

    def forward(t, values, yy, write):
        def block(i, carry):
            row = pl.multiple_of(i * MB, MB)
            out = jnp.dot(
                tiles[t, yy, pl.ds(row, MB), :],
                values[...].reshape(NX * W, 2 * W),
                preferred_element_type=F32,
            )
            write(row, out)
            return carry

        lax.fori_loop(0, NZ * W // MB, block, 0)

    def sep_dot(yy):
        def write(row, out):
            part[yy, pl.ds(row, MB), :] = out

        forward(0, leaf_all, yy, write)

    H = W // 2

    def reduce_col(p, ahead, lag, chunk, start_more, work, a_s, a_r, b_s, b_r, z_s, z_r):
        def zp_of(k):
            return lax.rem(z + order(k), NZ)

        def a_copies(k):
            return (
                remote(a_s.at[k, 0:H], a_r.at[0, k], a_ss.at[p, 0, k], a_rs.at[p, 0, k], to_up),
                remote(a_s.at[k, H:W], a_r.at[1, k], a_ss.at[p, 1, k], a_rs.at[p, 1, k], to_dn),
            )

        def b_copies(k):
            return (
                remote(b_s.at[0, k], b_r.at[0, k], b_ss.at[p, 0, k], b_rs.at[p, 0, k], to_up),
                remote(b_s.at[1, k], b_r.at[1, k], b_ss.at[p, 1, k], b_rs.at[p, 1, k], to_dn),
            )

        def z_copy(k):
            return remote(z_s.at[k], z_r.at[k], z_ss.at[p, k], z_rs.at[p, k], to_z(zp_of(k)))

        def send_a(k):
            a_s[k] = chunk(y_far, zp_of(k), 0, W).astype(BF)
            for copy in a_copies(k):
                copy.start()

        def send_b(k):
            zp = zp_of(k)
            up, dn = a_copies(k)
            cup, cdn = b_copies(k)
            b_s[0, k, H:W] = chunk(y_up, zp, H, H).astype(BF)
            b_s[1, k, 0:H] = chunk(y_dn, zp, 0, H).astype(BF)
            up.wait_recv()
            b_s[0, k, 0:H] = (chunk(y_up, zp, 0, H) + a_r[0, k].astype(F32)).astype(BF)
            cup.start()
            dn.wait_recv()
            b_s[1, k, H:W] = (chunk(y_dn, zp, H, H) + a_r[1, k].astype(F32)).astype(BF)
            cdn.start()

        def total(k):
            for copy in b_copies(k):
                copy.wait_recv()
            return chunk(y, zp_of(k), 0, W) + b_r[0, k].astype(F32) + b_r[1, k].astype(F32)

        def send_z(k):
            z_s[k] = total(k).astype(BF)
            z_copy(k).start()

        ahead = min(ahead, NZ)
        lag = min(lag, NZ - 1)
        for k in range(ahead):
            send_a(k)
        start_more()

        def step(k, carry):
            if ahead < NZ:

                @pl.when(k < NZ - ahead)
                def _():
                    send_a(k + ahead)

            send_b(k)
            work(k)

            @pl.when(k >= lag)
            def _():
                send_z(k - lag)

            return carry

        lax.fori_loop(0, NZ, step, 0)
        for k in range(max(0, NZ - lag), NZ - 1):
            send_z(k)
        out = total(NZ - 1)
        for k in range(NZ - 1):
            z_copy(k).wait_recv()
            out = out + z_r[k].astype(F32)

        def drain():
            def one(k, carry):
                for copy in a_copies(k) + b_copies(k):
                    copy.wait_send()

                @pl.when(k < NZ - 1)
                def _():
                    z_copy(k).wait_send()

                return carry

            lax.fori_loop(0, NZ, one, 0)

        return out, drain

    sep_dot(y_far)

    def sep_more():
        sep_dot(y_up)
        sep_dot(y_dn)
        sep_dot(y)

    def sep_chunk(yy, zp, lo, n):
        return part[yy, pl.ds(pl.multiple_of(zp * W + lo, n), n), :]

    per = max(1, 2 * NC // NZ)
    split = NZ // 2

    def top_leaf_dot(yy):
        def write(row, out):
            top_part[0, yy, pl.ds(row, MB), :] = out[:, 0:W]
            top_part[1, yy, pl.ds(row, MB), :] = out[:, W : 2 * W]

        forward(1, leaf_all, yy, write)

    def sep_work(k):
        @pl.when(k == 0)
        def _():
            loads[1].wait()
            loads[2].wait()

        @pl.when(k < split)
        def _():
            prep(1, tl_mask, k * per, per)

        @pl.when(k >= split)
        def _():
            prep(2, ts_mask, (k - split) * per, per)

        @pl.when(k == split)
        def _():
            top_leaf_dot(y)
            top_leaf_dot(y_up)

        @pl.when(k == NZ - 1)
        def _():
            top_leaf_dot(y_dn)
            top_leaf_dot(y_far)

    sep_sum, drain_sep = reduce_col(
        0, 4, 3, sep_chunk, sep_more, sep_work, fa_send, fa_recv, fb_send, fb_recv, fz_send, fz_recv
    )
    sy = jnp.dot(
        sep_inv[...],
        sep_rhs[...].astype(F32) - sep_sum,
        precision=HI,
        preferred_element_type=F32,
    )
    sep_y[...] = sy
    sep_all[x] = sy.astype(BF)
    sep_sends = x_gather(1, sep_all)
    for copy in sep_sends:
        copy.start()
    drain_sep()
    for copy in sep_sends:
        copy.wait()

    order_y = (y_far, y_up, y_dn, y)

    def swap_copy(i):
        return remote(
            swap_out.at[i], swap_in.at[i], swap_ss.at[i], swap_rs.at[i], to_pair
        )

    def top_dot(i):
        yy = order_y[i]

        def write(row, out):
            top_part[0, yy, pl.ds(row, MB), :] += out[:, 0:W]
            top_part[1, yy, pl.ds(row, MB), :] += out[:, W : 2 * W]
            swap_out[i, pl.ds(row, MB), :] = top_part[1 - s, yy, pl.ds(row, MB), :].astype(BF)

        forward(2, sep_all, yy, write)
        swap_copy(i).start()

    def join(i, yy):
        swap_copy(i).wait()

        def block(j, carry):
            row = pl.multiple_of(j * W, W)
            top_part[s, yy, pl.ds(row, W), :] += swap_in[i, pl.ds(row, W), :].astype(F32)
            return carry

        lax.fori_loop(0, NZ, block, 0)

    top_dot(0)
    top_dot(1)
    join(0, y_far)

    def top_more():
        top_dot(2)
        top_dot(3)
        join(1, y_up)
        join(2, y_dn)
        join(3, y)

    def top_chunk(yy, zp, lo, n):
        return top_part[s, yy, pl.ds(pl.multiple_of(zp * W + lo, n), n), :]

    top_sum, drain_top = reduce_col(
        1, 8, 5, top_chunk, top_more, lambda k: None, ta_send, ta_recv, tb_send, tb_recv, tz_send, tz_recv
    )
    mine = pl.ds(pl.multiple_of(s * W, W), W)
    ty = jnp.dot(
        top_inv[...],
        top_rhs[:, mine].astype(F32) - top_sum,
        precision=HI,
        preferred_element_type=F32,
    )
    tx = jnp.dot(ty.T, top_inv[...], precision=HI, preferred_element_type=F32)
    top_full[mine, :] = tx
    top_all[y, z, mine, :] = tx.astype(BF)

    def gather_col(p, buf, lo, rows, start_more, arrived, work, use, straight, behind, early):
        straight = max(0, NZ - straight)
        behind = min(behind, NZ - 1)
        done = max(0, NZ - early)

        def zp_of(k):
            return lax.rem(z + NZ - order(NZ - 1 - k), NZ)

        def at(yy, zz, first, n):
            return buf.at[yy, zz, pl.ds(pl.multiple_of(lo + first, n), n)]

        half = rows // 2

        def z_copy(k):
            ref = at(y, z, 0, rows)
            target = lax.rem(z + order(NZ - 1 - k), NZ)
            return remote(ref, ref, gz_ss.at[p, k], gz_rs.at[p, k], to_z(target))

        def z_arrival(k):
            ref = at(y, zp_of(k), 0, rows)
            target = lax.rem(z + order(NZ - 1 - k), NZ)
            return remote(ref, ref, gz_ss.at[p, k], gz_rs.at[p, k], to_z(target))

        def b_send(k):
            ref = at(y, zp_of(k), 0, rows)
            return (
                remote(ref, ref, gb_ss.at[p, 0, k], gb_rs.at[p, 0, k], to_up),
                remote(ref, ref, gb_ss.at[p, 1, k], gb_rs.at[p, 1, k], to_dn),
            )

        def b_arrival(k):
            from_dn = at(y_dn, zp_of(k), 0, rows)
            from_up = at(y_up, zp_of(k), 0, rows)
            return (
                remote(from_dn, from_dn, gb_ss.at[p, 0, k], gb_rs.at[p, 0, k], to_up),
                remote(from_up, from_up, gb_ss.at[p, 1, k], gb_rs.at[p, 1, k], to_dn),
            )

        def a_send(k):
            up = at(y_dn, zp_of(k), 0, half)
            dn = at(y_up, zp_of(k), half, half)
            return (
                remote(up, up, ga_ss.at[p, 0, k], ga_rs.at[p, 0, k], to_up),
                remote(dn, dn, ga_ss.at[p, 1, k], ga_rs.at[p, 1, k], to_dn),
            )

        def a_arrival(k):
            first = at(y_far, zp_of(k), 0, half)
            second = at(y_far, zp_of(k), half, half)
            return (
                remote(first, first, ga_ss.at[p, 0, k], ga_rs.at[p, 0, k], to_up),
                remote(second, second, ga_ss.at[p, 1, k], ga_rs.at[p, 1, k], to_dn),
            )

        def far_send(k):
            ref = at(y, zp_of(k), 0, rows)
            return remote(ref, ref, ga_ss.at[p, 0, k], ga_rs.at[p, 0, k], to_far)

        def far_arrival(k):
            ref = at(y_far, zp_of(k), 0, rows)
            return remote(ref, ref, ga_ss.at[p, 0, k], ga_rs.at[p, 0, k], to_far)

        def first_leg(k, wait):
            if wait:
                z_arrival(k).wait_recv()
            for copy in b_send(k):
                copy.start()

            @pl.when(k >= straight)
            def _():
                far_send(k).start()

            arrived(y, 0, zp_of(k), k)

        def second_leg(k):
            got = b_arrival(k)
            go = a_send(k)
            got[0].wait_recv()

            @pl.when(k < straight)
            def _():
                go[0].start()

            got[1].wait_recv()

            @pl.when(k < straight)
            def _():
                go[1].start()

            arrived(y_dn, 3, zp_of(k), k)
            arrived(y_up, 1, zp_of(k), k)

        def last_leg(k):
            @pl.when(k < straight)
            def _():
                for copy in a_arrival(k):
                    copy.wait_recv()

            @pl.when(k >= straight)
            def _():
                far_arrival(k).wait_recv()

            arrived(y_far, 2, zp_of(k), k)

        first_leg(0, False)
        for k in range(1, NZ):
            z_copy(k).start()
        start_more()
        work(zp_of(0))


        def step(k, carry):
            first_leg(k, True)
            work(zp_of(k))

            @pl.when(k >= behind)
            def _():
                second_leg(k - behind)

            if early < NZ:

                @pl.when(k >= early)
                def _():
                    last_leg(k - early)
                    use(zp_of(k - early), k - early)

            return carry

        lax.fori_loop(1, NZ, step, 0)
        for k in range(NZ - behind, NZ):
            second_leg(k)

        def finish(k, carry):
            last_leg(k)

            @pl.when(k >= done + 1)
            def _():
                use(zp_of(k - 1), k - 1)

            return carry

        lax.fori_loop(done, NZ, finish, 0)
        use(zp_of(NZ - 1), NZ - 1)

        def drain():
            def one(k, carry):
                for copy in b_send(k):
                    copy.wait_send()

                @pl.when(k < straight)
                def _():
                    for copy in a_send(k):
                        copy.wait_send()

                @pl.when(k >= straight)
                def _():
                    far_send(k).wait_send()

                return carry

            lax.fori_loop(0, NZ, one, 0)
            for k in range(1, NZ):
                z_copy(k).wait_send()

        return drain

    def backward(acc, buf, t, zz):
        for ya, yb in ((y, y_dn), (y_up, y_far)):
            left = jnp.concatenate([buf[ya, zz], buf[yb, zz]], axis=1)
            row = pl.ds(pl.multiple_of(zz * W, W), W)
            right = jnp.concatenate([tiles[t, ya, row, :], tiles[t, yb, row, :]], axis=0)
            acc[...] += jnp.dot(left, right, preferred_element_type=F32)

    other = pl.ds(pl.multiple_of((1 - s) * W, W), W)

    def pair_copy(yy, o, zz, k):
        ref = top_all.at[yy, zz, mine]
        return remote(ref, ref, pair_ss.at[o, k], pair_rs.at[o, k], to_pair)

    def pair_arrival(yy, o, zz, k):
        ref = top_all.at[yy, zz, other]
        return remote(ref, ref, pair_ss.at[o, k], pair_rs.at[o, k], to_pair)

    def top_arrived(yy, o, zz, k):
        pair_copy(yy, o, zz, k).start()

    full_copy = remote(
        top_full.at[mine], top_full.at[mine], full_ss.at[0], full_rs.at[0], to_pair
    )

    def top_start():
        full_copy.start()
        acc_sep[...] = jnp.zeros_like(acc_sep)
        acc_leaf[...] = jnp.zeros_like(acc_leaf)
        drain_top()

    def top_use(zz, k):
        for o, yy in enumerate((y, y_up, y_far, y_dn)):
            pair_arrival(yy, o, zz, k).wait_recv()
        backward(acc_sep, top_all, 2, zz)

    def no_work(zz):
        return None

    drain_gtop = gather_col(0, top_all, s * W, W, top_start, top_arrived, no_work, top_use, 4, 4, NZ)

    def x_reduce(p, acc):
        def copy(o):
            return remote(
                xr_send.at[p, o], xr_recv.at[p, o], xr_ss.at[p, o], xr_rs.at[p, o], to_x(o)
            )

        for o in range(1, NX):
            lane = pl.ds(pl.multiple_of(lax.rem(x + o, NX) * W, W), W)
            xr_send[p, o] = acc[:, lane].astype(BF)
            copy(o).start()
        out = acc[:, pl.ds(pl.multiple_of(x * W, W), W)]
        for o in range(1, NX):
            copy(o).wait_recv()
            out = out + xr_recv[p, o].astype(F32)

        def drain():
            for o in range(1, NX):
                copy(o).wait_send()

        return out, drain

    sep_t, drain_x0 = x_reduce(0, acc_sep)
    sx = jnp.dot(sep_y[...].T - sep_t, sep_inv[...], precision=HI, preferred_element_type=F32)
    sepx_all[y, z] = sx.astype(BF)

    def sep_start():
        sep_out[...] = sx
        drain_x0()
        drain_gtop()

        def one(k, carry):
            zz = lax.rem(z + NZ - order(NZ - 1 - k), NZ)
            for o, yy in enumerate((y, y_up, y_far, y_dn)):
                pair_copy(yy, o, zz, k).wait_send()
            return carry

        lax.fori_loop(0, NZ, one, 0)
        full_copy.wait()
        top_out[...] = top_full[...]

    def leaf_work(zz):
        backward(acc_leaf, top_all, 1, zz)

    def sep_use(zz, k):
        backward(acc_leaf, sepx_all, 0, zz)

    drain_gsep = gather_col(
        1, sepx_all, 0, 2 * W, sep_start, lambda yy, o, zz, k: None, leaf_work, sep_use, 2, 2, 5
    )
    leaf_t, drain_x1 = x_reduce(1, acc_leaf)
    leaf_out[...] = jnp.dot(
        leaf_y[...].T - leaf_t, leaf_inv[...], precision=HI, preferred_element_type=F32
    )
    drain_gsep()
    drain_x1()


def body(
    leaf_rhs,
    sep_rhs,
    top_rhs,
    leaf_inv,
    sep_inv,
    top_inv,
    sep_leaf,
    top_leaf,
    top_sep,
    sep_leaf_mask,
    top_leaf_mask,
    top_sep_mask,
):
    W = 128
    R = leaf_rhs.shape[-1]
    NC = sep_leaf.shape[2]
    NX = sep_leaf.shape[4]
    NZ = NC // NY
    rows = NC * W * NX

    def pattern(mask):
        return mask.reshape(NC, NX).T.reshape(NX, 1, NC)

    vm = pl.BlockSpec(memory_space=pltpu.VMEM)
    hbm = pl.BlockSpec(memory_space=pltpu.HBM)
    dma = pltpu.SemaphoreType.DMA
    out = jax.ShapeDtypeStruct((R, W), F32)
    H = W // 2

    def stage(cols):
        return [
            pltpu.VMEM((NZ, W, cols), BF),
            pltpu.VMEM((2, NZ, H, cols), BF),
            pltpu.VMEM((2, NZ, W, cols), BF),
            pltpu.VMEM((2, NZ, W, cols), BF),
            pltpu.VMEM((NZ, W, cols), BF),
            pltpu.VMEM((NZ, W, cols), BF),
        ]

    scratch = (
        [pltpu.VMEM((W, R), BF)] * 3
        + [pltpu.VMEM((W, W), F32)] * 3
        + [pltpu.SMEM((NX, 1, NC), jnp.int32)] * 3
        + [
            pltpu.VMEM((3, rows, W), BF),
            pltpu.VMEM((3, NY, NZ * W, NX * W), BF),
            pltpu.VMEM((64 * NX, 64 * NX), BF),
            pltpu.VMEM((W, R), F32),
            pltpu.VMEM((W, R), F32),
            pltpu.VMEM((NX, W, R), BF),
            pltpu.VMEM((NX, W, R), BF),
            pltpu.VMEM((NY, NZ * W, R), F32),
            pltpu.VMEM((2, NY, NZ * W, W), F32),
            pltpu.VMEM((NY, NZ * W, W), BF),
            pltpu.VMEM((NY, NZ * W, W), BF),
        ]
        + stage(R)
        + stage(W)
        + [
            pltpu.VMEM((R, W), F32),
            pltpu.VMEM((NY, NZ, R, W), BF),
            pltpu.VMEM((NY, NZ, R, W), BF),
            pltpu.VMEM((R, NX * W), F32),
            pltpu.VMEM((R, NX * W), F32),
            pltpu.VMEM((2, NX, R, W), BF),
            pltpu.VMEM((2, NX, R, W), BF),
            dma((3,)),
            dma((9,)),
        ]
        + [dma((2, NX))] * 4
        + [dma((2, 2, NZ))] * 4
        + [dma((2, NZ))] * 2
        + [dma((NY,))] * 2
        + [dma((2, 2, NZ))] * 4
        + [dma((2, NZ))] * 2
        + [dma((NY, NZ))] * 2
        + [dma((1,))] * 2
    )
    lx, sx, tx = pl.pallas_call(
        functools.partial(kernel, NX, NZ),
        out_shape=(out, out, out),
        in_specs=[hbm] * 12,
        out_specs=(vm, vm, vm),
        scratch_shapes=scratch,
        compiler_params=pltpu.CompilerParams(
            collective_id=0, has_side_effects=True, vmem_limit_bytes=50 * 1024 * 1024
        ),
    )(
        *(
            pltpu.with_memory_space_constraint(v, pltpu.HBM)
            for v in (
        leaf_rhs.reshape(W, R),
        sep_rhs.reshape(W, R),
        top_rhs.reshape(W, R),
        leaf_inv.reshape(W, W),
        sep_inv.reshape(W, W),
        top_inv.reshape(W, W),
        sep_leaf.reshape(rows, W),
        top_leaf.reshape(rows, W),
        top_sep.reshape(rows, W),
        pattern(sep_leaf_mask),
        pattern(top_leaf_mask),
        pattern(top_sep_mask),
            )
        )
    )
    return (lx.T[None, None, None, None], sx.T[None, None, None], tx.T[None, None])


def solution(mesh):
    in_specs = (
        P("sec", "row", None, "col", None, None),
        P("sec", "row", "col", None, None),
        P("row", "col", None, None),
        P("sec", "row", None, "col", None, None),
        P("sec", "row", "col", None, None),
        P("row", "col", None, None),
        P("sec", "row", None, None, None, None, "col", None),
        P("sec", "row", None, None, None, None, "col", None),
        P("sec", "row", None, None, None, "col", None),
        P("sec", "row", None, None, None, "col"),
        P("sec", "row", None, None, None, "col"),
        P("sec", "row", None, None, "col"),
    )
    out_specs = (
        P("sec", "row", None, "col", None, None),
        P("sec", "row", "col", None, None),
        P("row", "col", None, None),
    )
    return jax.shard_map(body, mesh=mesh, in_specs=in_specs, out_specs=out_specs, check_vma=False)
```

```python
import functools

import jax
import jax.numpy as jnp
from jax import lax
from jax.experimental import pallas as pl
from jax.experimental.pallas import tpu as pltpu
from jax.sharding import PartitionSpec as P

MESH = pl.DeviceIdType.MESH
NY = 4
BF = jnp.bfloat16
F32 = jnp.float32
HI = lax.Precision.HIGHEST


def kernel(
    NX,
    NZ,
    leaf_rhs_hbm,
    sep_rhs_hbm,
    top_rhs_hbm,
    leaf_inv_hbm,
    sep_inv_hbm,
    top_inv_hbm,
    sl_hbm,
    tl_hbm,
    ts_hbm,
    sl_mask_hbm,
    tl_mask_hbm,
    ts_mask_hbm,
    leaf_out,
    sep_out,
    top_out,
    leaf_rhs,
    sep_rhs,
    top_rhs,
    leaf_inv,
    sep_inv,
    top_inv,
    sl_mask,
    tl_mask,
    ts_mask,
    raw,
    tiles,
    select,
    leaf_y,
    sep_y,
    leaf_all,
    sep_all,
    part,
    top_part,
    swap_out,
    swap_in,
    fa_send,
    fa_recv,
    fb_send,
    fb_recv,
    fz_send,
    fz_recv,
    ta_send,
    ta_recv,
    tb_send,
    tb_recv,
    tz_send,
    tz_recv,
    top_full,
    top_all,
    sepx_all,
    acc_sep,
    acc_leaf,
    xr_send,
    xr_recv,
    load_sem,
    small_sem,
    xg_ss,
    xg_rs,
    xr_ss,
    xr_rs,
    a_ss,
    a_rs,
    b_ss,
    b_rs,
    z_ss,
    z_rs,
    swap_ss,
    swap_rs,
    ga_ss,
    ga_rs,
    gb_ss,
    gb_rs,
    gz_ss,
    gz_rs,
    pair_ss,
    pair_rs,
    full_ss,
    full_rs,
):
    W = 128
    NC = NY * NZ
    s = lax.axis_index("sec")
    x = lax.axis_index("row")
    c = lax.axis_index("col")
    z = c // NY
    y = c % NY

    def col_of(yy, zz):
        return zz * NY + yy

    y_up = lax.rem(y + 1, NY)
    y_far = lax.rem(y + 2, NY)
    y_dn = lax.rem(y + 3, NY)
    to_up = (s, x, col_of(y_up, z))
    to_dn = (s, x, col_of(y_dn, z))
    to_far = (s, x, col_of(y_far, z))
    to_pair = (1 - s, x, c)

    def to_x(o):
        return (s, lax.rem(x + o, NX), c)

    def to_z(zz):
        return (s, x, col_of(y, zz))

    def order(k):
        half = (k + 1) // 2
        return NZ // 2 + half * (1 - 2 * lax.rem(k, 2))

    def remote(src, dst, ss, rs, dev):
        return pltpu.make_async_remote_copy(
            src_ref=src,
            dst_ref=dst,
            send_sem=ss,
            recv_sem=rs,
            device_id=dev,
            device_id_type=MESH,
        )

    loads = [
        pltpu.make_async_copy(ref, raw.at[t], load_sem.at[t])
        for t, ref in enumerate((sl_hbm, tl_hbm, ts_hbm))
    ]
    small = [
        pltpu.make_async_copy(src, dst, small_sem.at[i])
        for i, (src, dst) in enumerate(
            (
                (leaf_rhs_hbm, leaf_rhs),
                (leaf_inv_hbm, leaf_inv),
                (sl_mask_hbm, sl_mask),
                (sep_rhs_hbm, sep_rhs),
                (sep_inv_hbm, sep_inv),
                (top_rhs_hbm, top_rhs),
                (top_inv_hbm, top_inv),
                (tl_mask_hbm, tl_mask),
                (ts_mask_hbm, ts_mask),
            )
        )
    ]
    for load in small[0:3]:
        load.start()
    loads[0].start()
    for load in small[3:]:
        load.start()

    barrier = pltpu.get_barrier_semaphore()

    def greet(dev):
        pl.semaphore_signal(barrier, inc=1, device_id=dev, device_id_type=MESH)

    greet(to_pair)
    for o in range(1, NX):
        greet(to_x(o))
    greet(to_up)
    greet(to_dn)
    greet(to_far)
    for o in range(1, NZ):
        greet(to_z(lax.rem(z + o, NZ)))

    small[0].wait()
    small[1].wait()
    ly = jnp.dot(leaf_inv[...], leaf_rhs[...].astype(F32), precision=HI, preferred_element_type=F32)
    leaf_y[...] = ly
    leaf_all[x] = ly.astype(BF)

    pl.semaphore_wait(barrier, NX + NZ + 2)

    def x_gather(p, buf):
        return [
            remote(buf.at[x], buf.at[x], xg_ss.at[p, o], xg_rs.at[p, o], to_x(o))
            for o in range(1, NX)
        ]

    leaf_sends = x_gather(0, leaf_all)
    for copy in leaf_sends:
        copy.start()

    SB = 64
    rows_i = lax.broadcasted_iota(jnp.int32, (SB * NX, SB * NX), 0)
    cols_i = lax.broadcasted_iota(jnp.int32, (SB * NX, SB * NX), 1)
    wanted = lax.rem(rows_i, SB) * NX + rows_i // SB
    select[...] = jnp.where(cols_i == wanted, 1.0, 0.0).astype(BF)

    def prep(t, mask, lo, n):
        def unit(i, carry):
            cc = lo + i
            yy = lax.rem(cc, NY)
            zz = cc // NY
            start = pl.multiple_of(cc * (W * NX), W * NX)
            block = jnp.concatenate(
                [raw[t, pl.ds(start + sub * (SB * NX), SB * NX), :] for sub in range(W // SB)],
                axis=1,
            )
            moved = jnp.dot(select[...], block, preferred_element_type=F32)
            for r in range(NX):
                keep = mask[r, 0, cc].astype(F32)
                for sub in range(W // SB):
                    row = pl.multiple_of(zz * W + sub * SB, SB)
                    tiles[t, yy, pl.ds(row, SB), r * W : (r + 1) * W] = (
                        moved[r * SB : (r + 1) * SB, sub * W : (sub + 1) * W] * keep
                    ).astype(BF)
            return carry

        lax.fori_loop(0, n, unit, 0)

    for load in small[2:]:
        load.wait()
    loads[0].wait()
    loads[1].start()
    loads[2].start()
    prep(0, sl_mask, 0, NC)

    for copy in leaf_sends:
        copy.wait()

    MB = min(512, NZ * W)

    def forward(t, values, yy, write):
        def block(i, carry):
            row = pl.multiple_of(i * MB, MB)
            out = jnp.dot(
                tiles[t, yy, pl.ds(row, MB), :],
                values[...].reshape(NX * W, 2 * W),
                preferred_element_type=F32,
            )
            write(row, out)
            return carry

        lax.fori_loop(0, NZ * W // MB, block, 0)

    def sep_dot(yy):
        def write(row, out):
            part[yy, pl.ds(row, MB), :] = out

        forward(0, leaf_all, yy, write)

    H = W // 2

    def reduce_col(p, ahead, lag, chunk, start_more, work, late, a_s, a_r, b_s, b_r, z_s, z_r):
        def zp_of(k):
            return lax.rem(z + order(k), NZ)

        def a_copies(k):
            return (
                remote(a_s.at[k, 0:H], a_r.at[0, k], a_ss.at[p, 0, k], a_rs.at[p, 0, k], to_up),
                remote(a_s.at[k, H:W], a_r.at[1, k], a_ss.at[p, 1, k], a_rs.at[p, 1, k], to_dn),
            )

        def b_copies(k):
            return (
                remote(b_s.at[0, k], b_r.at[0, k], b_ss.at[p, 0, k], b_rs.at[p, 0, k], to_up),
                remote(b_s.at[1, k], b_r.at[1, k], b_ss.at[p, 1, k], b_rs.at[p, 1, k], to_dn),
            )

        def z_copy(k):
            return remote(z_s.at[k], z_r.at[k], z_ss.at[p, k], z_rs.at[p, k], to_z(zp_of(k)))

        def send_a(k):
            a_s[k] = chunk(y_far, zp_of(k), 0, W).astype(BF)
            for copy in a_copies(k):
                copy.start()

        def send_b(k):
            zp = zp_of(k)
            up, dn = a_copies(k)
            cup, cdn = b_copies(k)
            b_s[0, k, H:W] = chunk(y_up, zp, H, H).astype(BF)
            b_s[1, k, 0:H] = chunk(y_dn, zp, 0, H).astype(BF)
            up.wait_recv()
            b_s[0, k, 0:H] = (chunk(y_up, zp, 0, H) + a_r[0, k].astype(F32)).astype(BF)
            cup.start()
            dn.wait_recv()
            b_s[1, k, H:W] = (chunk(y_dn, zp, H, H) + a_r[1, k].astype(F32)).astype(BF)
            cdn.start()

        def total(k):
            for copy in b_copies(k):
                copy.wait_recv()
            return chunk(y, zp_of(k), 0, W) + b_r[0, k].astype(F32) + b_r[1, k].astype(F32)

        def send_z(k):
            z_s[k] = total(k).astype(BF)
            z_copy(k).start()

        ahead = min(ahead, NZ)
        lag = min(lag, NZ - 1)
        for k in range(ahead):
            send_a(k)
        start_more()

        def step(k, carry):
            if ahead < NZ:

                @pl.when(k < NZ - ahead)
                def _():
                    send_a(k + ahead)

            send_b(k)
            work(k)

            @pl.when(k >= lag)
            def _():
                send_z(k - lag)

            return carry

        lax.fori_loop(0, NZ, step, 0)
        for k in range(max(0, NZ - lag), NZ - 1):
            send_z(k)
        late()
        out = total(NZ - 1)
        for k in range(NZ - 1):
            z_copy(k).wait_recv()
            out = out + z_r[k].astype(F32)

        def drain():
            def one(k, carry):
                for copy in a_copies(k) + b_copies(k):
                    copy.wait_send()

                @pl.when(k < NZ - 1)
                def _():
                    z_copy(k).wait_send()

                return carry

            lax.fori_loop(0, NZ, one, 0)

        return out, drain

    sep_dot(y_far)

    def sep_more():
        sep_dot(y_up)
        sep_dot(y_dn)
        sep_dot(y)

    def sep_chunk(yy, zp, lo, n):
        return part[yy, pl.ds(pl.multiple_of(zp * W + lo, n), n), :]

    per = max(1, 2 * NC // NZ)
    split = NZ // 2

    def top_leaf_dot(yy):
        def write(row, out):
            top_part[0, yy, pl.ds(row, MB), :] = out[:, 0:W]
            top_part[1, yy, pl.ds(row, MB), :] = out[:, W : 2 * W]

        forward(1, leaf_all, yy, write)

    def sep_work(k):
        @pl.when(k == 0)
        def _():
            loads[1].wait()
            loads[2].wait()

        @pl.when(k < split)
        def _():
            prep(1, tl_mask, k * per, per)

        @pl.when(k >= split)
        def _():
            prep(2, ts_mask, (k - split) * per, per)

        @pl.when(k == split)
        def _():
            top_leaf_dot(y)
            top_leaf_dot(y_up)

    def sep_late():
        top_leaf_dot(y_dn)
        top_leaf_dot(y_far)

    sep_sum, drain_sep = reduce_col(
        0, 4, 3, sep_chunk, sep_more, sep_work, sep_late, fa_send, fa_recv, fb_send, fb_recv, fz_send, fz_recv
    )
    sy = jnp.dot(
        sep_inv[...],
        sep_rhs[...].astype(F32) - sep_sum,
        precision=HI,
        preferred_element_type=F32,
    )
    sep_y[...] = sy
    sep_all[x] = sy.astype(BF)
    sep_sends = x_gather(1, sep_all)
    for copy in sep_sends:
        copy.start()
    drain_sep()
    for copy in sep_sends:
        copy.wait()

    order_y = (y_far, y_up, y_dn, y)

    def swap_copy(i):
        return remote(
            swap_out.at[i], swap_in.at[i], swap_ss.at[i], swap_rs.at[i], to_pair
        )

    def top_dot(i):
        yy = order_y[i]

        def write(row, out):
            top_part[0, yy, pl.ds(row, MB), :] += out[:, 0:W]
            top_part[1, yy, pl.ds(row, MB), :] += out[:, W : 2 * W]
            swap_out[i, pl.ds(row, MB), :] = top_part[1 - s, yy, pl.ds(row, MB), :].astype(BF)

        forward(2, sep_all, yy, write)
        swap_copy(i).start()

    def join(i, yy):
        swap_copy(i).wait()

        def block(j, carry):
            row = pl.multiple_of(j * W, W)
            top_part[s, yy, pl.ds(row, W), :] += swap_in[i, pl.ds(row, W), :].astype(F32)
            return carry

        lax.fori_loop(0, NZ, block, 0)

    top_dot(0)
    top_dot(1)
    join(0, y_far)

    def top_more():
        top_dot(2)
        top_dot(3)
        join(1, y_up)
        join(2, y_dn)
        join(3, y)

    def top_chunk(yy, zp, lo, n):
        return top_part[s, yy, pl.ds(pl.multiple_of(zp * W + lo, n), n), :]

    top_sum, drain_top = reduce_col(
        1, 8, 5, top_chunk, top_more, lambda k: None, lambda: None, ta_send, ta_recv, tb_send, tb_recv, tz_send, tz_recv
    )
    mine = pl.ds(pl.multiple_of(s * W, W), W)
    ty = jnp.dot(
        top_inv[...],
        top_rhs[:, mine].astype(F32) - top_sum,
        precision=HI,
        preferred_element_type=F32,
    )
    tx = jnp.dot(ty.T, top_inv[...], precision=HI, preferred_element_type=F32)
    top_full[mine, :] = tx
    top_all[y, z, mine, :] = tx.astype(BF)

    def gather_col(p, buf, lo, rows, start_more, arrived, work, use, straight, behind, early):
        straight = max(0, NZ - straight)
        behind = min(behind, NZ - 1)
        done = max(0, NZ - early)

        def zp_of(k):
            return lax.rem(z + NZ - order(NZ - 1 - k), NZ)

        def at(yy, zz, first, n):
            return buf.at[yy, zz, pl.ds(pl.multiple_of(lo + first, n), n)]

        half = rows // 2

        def z_copy(k):
            ref = at(y, z, 0, rows)
            target = lax.rem(z + order(NZ - 1 - k), NZ)
            return remote(ref, ref, gz_ss.at[p, k], gz_rs.at[p, k], to_z(target))

        def z_arrival(k):
            ref = at(y, zp_of(k), 0, rows)
            target = lax.rem(z + order(NZ - 1 - k), NZ)
            return remote(ref, ref, gz_ss.at[p, k], gz_rs.at[p, k], to_z(target))

        def b_send(k):
            ref = at(y, zp_of(k), 0, rows)
            return (
                remote(ref, ref, gb_ss.at[p, 0, k], gb_rs.at[p, 0, k], to_up),
                remote(ref, ref, gb_ss.at[p, 1, k], gb_rs.at[p, 1, k], to_dn),
            )

        def b_arrival(k):
            from_dn = at(y_dn, zp_of(k), 0, rows)
            from_up = at(y_up, zp_of(k), 0, rows)
            return (
                remote(from_dn, from_dn, gb_ss.at[p, 0, k], gb_rs.at[p, 0, k], to_up),
                remote(from_up, from_up, gb_ss.at[p, 1, k], gb_rs.at[p, 1, k], to_dn),
            )

        def a_send(k):
            up = at(y_dn, zp_of(k), 0, half)
            dn = at(y_up, zp_of(k), half, half)
            return (
                remote(up, up, ga_ss.at[p, 0, k], ga_rs.at[p, 0, k], to_up),
                remote(dn, dn, ga_ss.at[p, 1, k], ga_rs.at[p, 1, k], to_dn),
            )

        def a_arrival(k):
            first = at(y_far, zp_of(k), 0, half)
            second = at(y_far, zp_of(k), half, half)
            return (
                remote(first, first, ga_ss.at[p, 0, k], ga_rs.at[p, 0, k], to_up),
                remote(second, second, ga_ss.at[p, 1, k], ga_rs.at[p, 1, k], to_dn),
            )

        def far_send(k):
            ref = at(y, zp_of(k), 0, rows)
            return remote(ref, ref, ga_ss.at[p, 0, k], ga_rs.at[p, 0, k], to_far)

        def far_arrival(k):
            ref = at(y_far, zp_of(k), 0, rows)
            return remote(ref, ref, ga_ss.at[p, 0, k], ga_rs.at[p, 0, k], to_far)

        def first_leg(k, wait):
            if wait:
                z_arrival(k).wait_recv()
            for copy in b_send(k):
                copy.start()

            @pl.when(k >= straight)
            def _():
                far_send(k).start()

            arrived(y, 0, zp_of(k), k)

        def second_leg(k):
            got = b_arrival(k)
            go = a_send(k)
            got[0].wait_recv()

            @pl.when(k < straight)
            def _():
                go[0].start()

            got[1].wait_recv()

            @pl.when(k < straight)
            def _():
                go[1].start()

            arrived(y_dn, 3, zp_of(k), k)
            arrived(y_up, 1, zp_of(k), k)

        def last_leg(k):
            @pl.when(k < straight)
            def _():
                for copy in a_arrival(k):
                    copy.wait_recv()

            @pl.when(k >= straight)
            def _():
                far_arrival(k).wait_recv()

            arrived(y_far, 2, zp_of(k), k)

        first_leg(0, False)
        for k in range(1, NZ):
            z_copy(k).start()
        start_more()
        work(zp_of(0))


        def step(k, carry):
            first_leg(k, True)
            work(zp_of(k))

            @pl.when(k >= behind)
            def _():
                second_leg(k - behind)

            if early < NZ:

                @pl.when(k >= early)
                def _():
                    last_leg(k - early)
                    use(zp_of(k - early), k - early)

            return carry

        lax.fori_loop(1, NZ, step, 0)
        for k in range(NZ - behind, NZ):
            second_leg(k)

        def finish(k, carry):
            last_leg(k)

            @pl.when(k >= done + 1)
            def _():
                use(zp_of(k - 1), k - 1)

            return carry

        lax.fori_loop(done, NZ, finish, 0)
        use(zp_of(NZ - 1), NZ - 1)

        def drain():
            def one(k, carry):
                for copy in b_send(k):
                    copy.wait_send()

                @pl.when(k < straight)
                def _():
                    for copy in a_send(k):
                        copy.wait_send()

                @pl.when(k >= straight)
                def _():
                    far_send(k).wait_send()

                return carry

            lax.fori_loop(0, NZ, one, 0)
            for k in range(1, NZ):
                z_copy(k).wait_send()

        return drain

    def backward(acc, buf, t, zz):
        for ya, yb in ((y, y_dn), (y_up, y_far)):
            left = jnp.concatenate([buf[ya, zz], buf[yb, zz]], axis=1)
            row = pl.ds(pl.multiple_of(zz * W, W), W)
            right = jnp.concatenate([tiles[t, ya, row, :], tiles[t, yb, row, :]], axis=0)
            acc[...] += jnp.dot(left, right, preferred_element_type=F32)

    other = pl.ds(pl.multiple_of((1 - s) * W, W), W)

    def pair_copy(yy, o, zz, k):
        ref = top_all.at[yy, zz, mine]
        return remote(ref, ref, pair_ss.at[o, k], pair_rs.at[o, k], to_pair)

    def pair_arrival(yy, o, zz, k):
        ref = top_all.at[yy, zz, other]
        return remote(ref, ref, pair_ss.at[o, k], pair_rs.at[o, k], to_pair)

    def top_arrived(yy, o, zz, k):
        pair_copy(yy, o, zz, k).start()

    full_copy = remote(
        top_full.at[mine], top_full.at[mine], full_ss.at[0], full_rs.at[0], to_pair
    )

    def top_start():
        full_copy.start()
        acc_sep[...] = jnp.zeros_like(acc_sep)
        acc_leaf[...] = jnp.zeros_like(acc_leaf)
        drain_top()

    def top_use(zz, k):
        for o, yy in enumerate((y, y_up, y_far, y_dn)):
            pair_arrival(yy, o, zz, k).wait_recv()
        backward(acc_sep, top_all, 2, zz)

    def no_work(zz):
        return None

    drain_gtop = gather_col(0, top_all, s * W, W, top_start, top_arrived, no_work, top_use, 4, 4, NZ)

    def x_reduce(p, acc):
        def copy(o):
            return remote(
                xr_send.at[p, o], xr_recv.at[p, o], xr_ss.at[p, o], xr_rs.at[p, o], to_x(o)
            )

        for o in range(1, NX):
            lane = pl.ds(pl.multiple_of(lax.rem(x + o, NX) * W, W), W)
            xr_send[p, o] = acc[:, lane].astype(BF)
            copy(o).start()
        out = acc[:, pl.ds(pl.multiple_of(x * W, W), W)]
        for o in range(1, NX):
            copy(o).wait_recv()
            out = out + xr_recv[p, o].astype(F32)

        def drain():
            for o in range(1, NX):
                copy(o).wait_send()

        return out, drain

    sep_t, drain_x0 = x_reduce(0, acc_sep)
    sx = jnp.dot(sep_y[...].T - sep_t, sep_inv[...], precision=HI, preferred_element_type=F32)
    sepx_all[y, z] = sx.astype(BF)

    def sep_start():
        sep_out[...] = sx
        drain_x0()
        drain_gtop()

        def one(k, carry):
            zz = lax.rem(z + NZ - order(NZ - 1 - k), NZ)
            for o, yy in enumerate((y, y_up, y_far, y_dn)):
                pair_copy(yy, o, zz, k).wait_send()
            return carry

        lax.fori_loop(0, NZ, one, 0)
        full_copy.wait()
        top_out[...] = top_full[...]

    def leaf_work(zz):
        backward(acc_leaf, top_all, 1, zz)

    def sep_use(zz, k):
        backward(acc_leaf, sepx_all, 0, zz)

    drain_gsep = gather_col(
        1, sepx_all, 0, 2 * W, sep_start, lambda yy, o, zz, k: None, leaf_work, sep_use, 2, 2, 5
    )
    leaf_t, drain_x1 = x_reduce(1, acc_leaf)
    leaf_out[...] = jnp.dot(
        leaf_y[...].T - leaf_t, leaf_inv[...], precision=HI, preferred_element_type=F32
    )
    drain_gsep()
    drain_x1()


def body(
    leaf_rhs,
    sep_rhs,
    top_rhs,
    leaf_inv,
    sep_inv,
    top_inv,
    sep_leaf,
    top_leaf,
    top_sep,
    sep_leaf_mask,
    top_leaf_mask,
    top_sep_mask,
):
    W = 128
    R = leaf_rhs.shape[-1]
    NC = sep_leaf.shape[2]
    NX = sep_leaf.shape[4]
    NZ = NC // NY
    rows = NC * W * NX

    def pattern(mask):
        return mask.reshape(NC, NX).T.reshape(NX, 1, NC)

    vm = pl.BlockSpec(memory_space=pltpu.VMEM)
    hbm = pl.BlockSpec(memory_space=pltpu.HBM)
    dma = pltpu.SemaphoreType.DMA
    out = jax.ShapeDtypeStruct((R, W), F32)
    H = W // 2

    def stage(cols):
        return [
            pltpu.VMEM((NZ, W, cols), BF),
            pltpu.VMEM((2, NZ, H, cols), BF),
            pltpu.VMEM((2, NZ, W, cols), BF),
            pltpu.VMEM((2, NZ, W, cols), BF),
            pltpu.VMEM((NZ, W, cols), BF),
            pltpu.VMEM((NZ, W, cols), BF),
        ]

    scratch = (
        [pltpu.VMEM((W, R), BF)] * 3
        + [pltpu.VMEM((W, W), F32)] * 3
        + [pltpu.SMEM((NX, 1, NC), jnp.int32)] * 3
        + [
            pltpu.VMEM((3, rows, W), BF),
            pltpu.VMEM((3, NY, NZ * W, NX * W), BF),
            pltpu.VMEM((64 * NX, 64 * NX), BF),
            pltpu.VMEM((W, R), F32),
            pltpu.VMEM((W, R), F32),
            pltpu.VMEM((NX, W, R), BF),
            pltpu.VMEM((NX, W, R), BF),
            pltpu.VMEM((NY, NZ * W, R), F32),
            pltpu.VMEM((2, NY, NZ * W, W), F32),
            pltpu.VMEM((NY, NZ * W, W), BF),
            pltpu.VMEM((NY, NZ * W, W), BF),
        ]
        + stage(R)
        + stage(W)
        + [
            pltpu.VMEM((R, W), F32),
            pltpu.VMEM((NY, NZ, R, W), BF),
            pltpu.VMEM((NY, NZ, R, W), BF),
            pltpu.VMEM((R, NX * W), F32),
            pltpu.VMEM((R, NX * W), F32),
            pltpu.VMEM((2, NX, R, W), BF),
            pltpu.VMEM((2, NX, R, W), BF),
            dma((3,)),
            dma((9,)),
        ]
        + [dma((2, NX))] * 4
        + [dma((2, 2, NZ))] * 4
        + [dma((2, NZ))] * 2
        + [dma((NY,))] * 2
        + [dma((2, 2, NZ))] * 4
        + [dma((2, NZ))] * 2
        + [dma((NY, NZ))] * 2
        + [dma((1,))] * 2
    )
    lx, sx, tx = pl.pallas_call(
        functools.partial(kernel, NX, NZ),
        out_shape=(out, out, out),
        in_specs=[hbm] * 12,
        out_specs=(vm, vm, vm),
        scratch_shapes=scratch,
        compiler_params=pltpu.CompilerParams(
            collective_id=0, has_side_effects=True, vmem_limit_bytes=50 * 1024 * 1024
        ),
    )(
        *(
            pltpu.with_memory_space_constraint(v, pltpu.HBM)
            for v in (
        leaf_rhs.reshape(W, R),
        sep_rhs.reshape(W, R),
        top_rhs.reshape(W, R),
        leaf_inv.reshape(W, W),
        sep_inv.reshape(W, W),
        top_inv.reshape(W, W),
        sep_leaf.reshape(rows, W),
        top_leaf.reshape(rows, W),
        top_sep.reshape(rows, W),
        pattern(sep_leaf_mask),
        pattern(top_leaf_mask),
        pattern(top_sep_mask),
            )
        )
    )
    return (lx.T[None, None, None, None], sx.T[None, None, None], tx.T[None, None])


def solution(mesh):
    in_specs = (
        P("sec", "row", None, "col", None, None),
        P("sec", "row", "col", None, None),
        P("row", "col", None, None),
        P("sec", "row", None, "col", None, None),
        P("sec", "row", "col", None, None),
        P("row", "col", None, None),
        P("sec", "row", None, None, None, None, "col", None),
        P("sec", "row", None, None, None, None, "col", None),
        P("sec", "row", None, None, None, "col", None),
        P("sec", "row", None, None, None, "col"),
        P("sec", "row", None, None, None, "col"),
        P("sec", "row", None, None, "col"),
    )
    out_specs = (
        P("sec", "row", None, "col", None, None),
        P("sec", "row", "col", None, None),
        P("row", "col", None, None),
    )
    return jax.shard_map(body, mesh=mesh, in_specs=in_specs, out_specs=out_specs, check_vma=False)
```
